32 devices in a mesh: corpus: 4 (over y, x), fsdp: 8 (over z, core).
Axes of the slice: x: 2, y: 2, z: 4, core: 2. Of those that a mesh axis runs over, the one named last changes fastest.
Arguments:
- inputs: bfloat16 [2048, 4096], P('fsdp', 'corpus'), may hold values from -128 to 128
- norm_gain: float32 [4096], replicated, may hold values from 0.1 to 1.9
- w_query: bfloat16 [4096, 8192], P('fsdp', 'corpus'), may hold values from -0.09375 to 0.09375
- w_key: bfloat16 [4096, 1024], P('fsdp', 'corpus'), may hold values from -0.09375 to 0.09375
- w_value: bfloat16 [4096, 1024], P('fsdp', 'corpus'), may hold values from -0.375 to 0.375
- query_bias: float32 [8192], P('corpus'), may hold values from -16 to 16
- key_bias: float32 [1024], P('corpus'), may hold values from -16 to 16
- value_bias: float32 [1024], P('corpus'), may hold values from -4 to 4
- key_cache: bfloat16 [8, 2048, 1024], P('fsdp', None, 'corpus'), may hold values from -16 to 16
- value_cache: bfloat16 [8, 2048, 1024], P('fsdp', None, 'corpus'), may hold values from -16 to 16
- source_doc: int32 [32], P('fsdp'), may hold values from 0 to 7, as said below
- prefix_len: int32 [32], P('fsdp'), may hold values from 1 to 2048
Outputs:
- attention: bfloat16 [2048, 8192], P('fsdp', 'corpus')
The draws below stay inside these ranges and needn't reach their ends.
Inputs may be any that keep to these rules, and one draw needn't show every extreme that they name: `source_doc`: within the suffixes of one index of fsdp (aligned blocks of 4) no document appears more than 2 times, and one document, drawn from the seed, appears exactly 2 times in every such block.
All inputs are finite; a program needn't handle non-finite values.
Results may differ from the reference program's by a relative error of at most 0.0075.
The reference program's roundings to bfloat16 on the way (of `normed`, `own_values`, `queries`, `own_keys` and `prefix_normed`) count: a program that leaves them out, or rounds other values in their place, can miss the bound.
Values may be sent and summed in bfloat16 or wider, within the bound.
A program may use at most 128 MiB of HBM per device.

```python
import jax
import jax.numpy as jnp
from jax import lax

D = 4096
HQ = 64
KVH = 8
HD = 128
SL = 64
DOCLEN = 2048
CAP = 2
SUF_DEV = 4
SUFFIXES = 32
TOKENS = 2048
DOCS = 8


def draw_inputs(key, part):
    row_scale = 10.0 ** jax.random.uniform(jax.random.fold_in(key, 1), (TOKENS, 1), jnp.float32, 0.0, 1.0)
    column_scale = 10.0 ** jax.random.uniform(jax.random.fold_in(key, 2), (1, D), jnp.float32, -0.5, 0.5)
    base = jnp.clip(jax.random.normal(jax.random.fold_in(key, 3), (TOKENS, D), jnp.float32), -4.0, 4.0)
    return (base * row_scale * column_scale).astype(jnp.bfloat16)


def draw_query_bias(key, part):
    noise = jnp.clip(0.5 * jax.random.normal(jax.random.fold_in(key, 11), (HQ, HD), jnp.float32), -3.0, 3.0)
    return noise.reshape(HQ * HD)


def draw_key_bias(key, part):
    noise = jnp.clip(0.5 * jax.random.normal(jax.random.fold_in(key, 12), (KVH, HD), jnp.float32), -3.0, 3.0)
    return noise.reshape(KVH * HD)


def draw_key_cache(key, part):
    shape = (DOCS, DOCLEN, KVH, HD)
    base = jnp.clip(jax.random.normal(jax.random.fold_in(key, 21), shape, jnp.float32), -6.0, 6.0)
    return base.reshape(DOCS, DOCLEN, KVH * HD).astype(jnp.bfloat16)


def draw_source_doc(key, part):
    readers = SUFFIXES // SUF_DEV
    favored = jax.random.randint(jax.random.fold_in(key, 5), (), 0, DOCS)

    def one_reader(index):
        local_key = jax.random.fold_in(key, 1000 + index)
        others = jnp.arange((DOCS - 1) * CAP, dtype=jnp.int32) // CAP
        others = others + (others >= favored).astype(jnp.int32)
        mixed = jax.random.permutation(jax.random.fold_in(local_key, 1), others)
        picks = jnp.concatenate([jnp.full((CAP,), favored, jnp.int32), mixed[:SUF_DEV - CAP]])
        return jax.random.permutation(jax.random.fold_in(local_key, 2), picks)
    return jax.vmap(one_reader)(jnp.arange(readers, dtype=jnp.int32)).reshape(SUFFIXES)


def touch_ends(array, key, low, top_value):
    index_at = [jax.random.randint(jax.random.fold_in(key, axis), (), 0, length) for axis, length in enumerate(array.shape)]
    main_axis = array.shape.index(max(array.shape))
    neighbour = index_at[:main_axis] + [(index_at[main_axis] + 1) % array.shape[main_axis]] + index_at[main_axis + 1:]
    return array.at[tuple(index_at)].set(low).at[tuple(neighbour)].set(top_value)


def block_levels(own_key, extent, split, least, largest):
    loudness, own = 1.0, jax.random.fold_in(own_key, 6)
    for dim, shards_of in split:
        heights = jnp.exp(jax.random.uniform(jax.random.fold_in(own, dim), (shards_of,), jnp.float32, least / len(split), largest / len(split)))
        loudness = loudness * jnp.repeat(heights, extent[dim] // shards_of).reshape([-1 if axis == dim else 1 for axis in range(len(extent))])
    return loudness


def scatter_about(key, dims, deviation, reach, cuts=(), kind=jnp.bfloat16):
    loudness = block_levels(key, dims, cuts, -0.22, 0.18) if cuts else 1.0
    values = jax.random.normal(key, dims, jnp.float32) * deviation * loudness
    return jnp.minimum(jnp.maximum(values, -reach), reach).astype(kind)


def setup_inputs(seed: int = 0) -> dict:
    seeds = jax.random.split(jax.random.key(seed), 13)
    return {
        "inputs": draw_inputs(jax.random.fold_in(seeds[12], 71), 0),
        "norm_gain": jnp.clip(1.0 + 0.18 * jax.random.normal(seeds[1], (D,), jnp.float32), 0.1, 1.9),
        "w_query": scatter_about(seeds[2], (D, HQ * HD), D ** -0.5, 0.09375, ((0, 8), (1, 4))),
        "w_key": scatter_about(seeds[3], (D, KVH * HD), D ** -0.5, 0.09375, ((0, 8), (1, 4))),
        "w_value": scatter_about(seeds[4], (D, KVH * HD), (D // 16) ** -0.5, 0.375, ((0, 8), (1, 4))),
        "query_bias": draw_query_bias(jax.random.fold_in(seeds[12], 71), 0),
        "key_bias": draw_key_bias(jax.random.fold_in(seeds[12], 71), 0),
        "value_bias": scatter_about(seeds[7], (KVH * HD,), 1.0, 4.0, ((0, 4),), jnp.float32),
        "key_cache": draw_key_cache(jax.random.fold_in(seeds[12], 71), 0),
        "value_cache": scatter_about(seeds[9], (DOCS, DOCLEN, KVH * HD), 4.0, 16.0, ((0, 8), (2, 4))),
        "source_doc": draw_source_doc(jax.random.fold_in(seeds[12], 71), 0),
        "prefix_len": touch_ends(jax.random.randint(seeds[11], (SUFFIXES,), 1, DOCLEN + 1), jax.random.fold_in(seeds[11], 1), 1, DOCLEN).astype(jnp.int32),
    }


EPS = 1e-06
THETA = 1000000.0
MASKED = -1e+30

def rope_tables(position, width):
    half = width // 2
    freq = THETA ** (-(jnp.arange(half, dtype=jnp.float32) * 2.0 / width))
    angle = position.astype(jnp.float32)[..., None] * freq
    angle = jnp.concatenate([angle, angle], axis=-1)
    return (jnp.cos(angle), jnp.sin(angle))

def rotate(vector, cosine, sine):
    half = vector.shape[-1] // 2
    turned = jnp.concatenate([-vector[..., half:], vector[..., :half]], axis=-1)
    return vector * cosine + turned * sine

def normalize(rows, norm_gain):
    wide = rows.astype(jnp.float32)
    spread = lax.optimization_barrier(jnp.mean(wide * wide, axis=-1, keepdims=True))
    return (wide * lax.rsqrt(spread + EPS) * norm_gain).astype(jnp.bfloat16)

def partial_attend(query, keys, values, live):
    count = query.shape[0]
    width = query.shape[2]
    length = keys.shape[0]
    kv_heads = keys.shape[1] // width
    group = query.shape[1] // kv_heads
    grouped = query.reshape(count, kv_heads, group, width).astype(jnp.float32)
    key_rows = keys.reshape(length, kv_heads, width).astype(jnp.float32)
    scores = jnp.einsum('tkgd,lkd->tkgl', grouped, key_rows) * width ** (-0.5)
    scores = jnp.where(live[:, None, None, :], scores, MASKED)
    peak = lax.optimization_barrier(jnp.max(scores, axis=-1))
    weights = jnp.exp(scores - peak[..., None])
    total = lax.optimization_barrier(jnp.sum(weights, axis=-1))
    rounded = weights.astype(jnp.bfloat16).astype(jnp.float32)
    value_rows = values.reshape(length, kv_heads, width).astype(jnp.float32)
    weighted = jnp.einsum('tkgl,lkd->tkgd', rounded, value_rows)
    return (weighted.reshape(count, kv_heads * group * width), peak.reshape(count, kv_heads * group), total.reshape(count, kv_heads * group))

def settle(part):
    weighted, peak, total = part
    shape = peak.shape + (-1,)
    normed = (weighted.reshape(shape) / total[..., None]).reshape(weighted.shape).astype(jnp.bfloat16)
    return (normed, peak + jnp.log(total))

def combine(prefix_normed, prefix_lse, own):
    own_out, own_peak, own_total = own
    top = jnp.maximum(prefix_lse, own_peak)
    scale_first = jnp.exp(prefix_lse - top)
    scale_second = jnp.exp(own_peak - top)
    divisor = scale_first + own_total * scale_second
    shape = own_peak.shape + (-1,)
    mixed = prefix_normed.astype(jnp.float32).reshape(shape) * scale_first[..., None] + own_out.reshape(shape) * scale_second[..., None]
    mixed = mixed / divisor[..., None]
    return mixed.reshape(own_peak.shape[:-1] + (-1,)).astype(jnp.bfloat16)

def reference(inputs, norm_gain, w_query, w_key, w_value, query_bias, key_bias, value_bias, key_cache, value_cache, source_doc, prefix_len):
    blocks = inputs.reshape(SUFFIXES, SL, D)

    def one_suffix(item):
        rows, document, length = item
        normed = normalize(rows, norm_gain)
        query_lin = jnp.dot(normed, w_query, preferred_element_type=jnp.float32) + query_bias
        key_lin = jnp.dot(normed, w_key, preferred_element_type=jnp.float32) + key_bias
        own_values = (jnp.dot(normed, w_value, preferred_element_type=jnp.float32) + value_bias).astype(jnp.bfloat16)
        position = length + jnp.arange(SL, dtype=jnp.int32)
        cosine, sine = rope_tables(position, HD)
        queries = rotate(query_lin.reshape(SL, HQ, HD), cosine[:, None, :], sine[:, None, :]).astype(jnp.bfloat16)
        own_keys = rotate(key_lin.reshape(SL, KVH, HD), cosine[:, None, :], sine[:, None, :]).astype(jnp.bfloat16)
        doc_keys = lax.dynamic_index_in_dim(key_cache, document, 0, keepdims=False)
        doc_values = lax.dynamic_index_in_dim(value_cache, document, 0, keepdims=False)
        prefix_live = jnp.broadcast_to(jnp.arange(DOCLEN, dtype=jnp.int32)[None, :] < length, (SL, DOCLEN))
        causal = jnp.arange(SL, dtype=jnp.int32)[None, :] <= jnp.arange(SL, dtype=jnp.int32)[:, None]
        prefix_normed, prefix_lse = settle(partial_attend(queries, doc_keys, doc_values, prefix_live))
        own_part = partial_attend(queries, own_keys.reshape(SL, KVH * HD), own_values, causal)
        return combine(prefix_normed, prefix_lse, own_part)
    result = lax.map(one_suffix, (blocks, source_doc, prefix_len))
    return result.reshape(TOKENS, HQ * HD)
```

```python
import functools

import jax
import jax.numpy as jnp
from jax import lax
from jax.experimental import pallas as pl
from jax.experimental.pallas import tpu as pltpu
from jax.sharding import PartitionSpec as P

HD = 128
SL = 64
EPS = 1e-06
THETA = 1000000.0
MASKED = -1e30
KEY_BLOCK = 512
MESH = pl.DeviceIdType.MESH
LINES = 4
COLUMNS = 4


def rope_tables(position, width):
    half = width // 2
    freq = THETA ** (-(jnp.arange(half, dtype=jnp.float32) * 2.0 / width))
    angle = position.astype(jnp.float32)[..., None] * freq
    cosine, sine = jnp.cos(angle), jnp.sin(angle)
    return (
        jnp.concatenate([cosine, cosine], axis=-1),
        jnp.concatenate([-sine, sine], axis=-1),
    )


def normalize(rows, norm_gain):
    wide = rows.astype(jnp.float32)
    spread = jnp.mean(wide * wide, axis=-1, keepdims=True)
    return (wide * lax.rsqrt(spread + EPS) * norm_gain).astype(jnp.bfloat16)


def rotate(vector, cosine, sine):
    return vector * cosine + pltpu.roll(vector, HD // 2, 1) * sine


def over_lanes(op, array):
    parts = [array[:, at : at + 128] for at in range(0, array.shape[1], 128)]
    while len(parts) > 1:
        parts = [op(a, b) for a, b in zip(parts[::2], parts[1::2])]
    return parts[0]


def attend_kernel(
    doc_ref,
    len_ref,
    q_ref,
    k_ref,
    v_ref,
    keys_ref,
    values_ref,
    out_ref,
    scores_ref,
    peak_ref,
    total_ref,
    acc_ref,
):
    suffix = pl.program_id(0)
    length = len_ref[suffix]
    scale = HD ** (-0.5)
    rows = q_ref.shape[1]
    group = rows // SL
    own_keys = k_ref[0]
    own_values = v_ref[0]
    dims = (((1,), (1,)), ((), ()))

    block = KEY_BLOCK
    blocks = lax.div(length + (block - 1), block)
    peak_ref[...] = jnp.full(peak_ref.shape, MASKED, jnp.float32)

    @pl.loop(0, blocks)
    def _(b):
        at = pl.multiple_of(b * block, block)
        scores = lax.dot_general(
            q_ref[0],
            keys_ref[0, pl.ds(at, block), :],
            dims,
            preferred_element_type=jnp.float32,
        ) * scale
        column = lax.broadcasted_iota(jnp.int32, (1, block), 1) + at
        scores = jnp.where(column < length, scores, MASKED)
        scores_ref[b] = scores
        peak_ref[...] = jnp.maximum(peak_ref[...], over_lanes(jnp.maximum, scores))

    peak = jnp.max(peak_ref[...], axis=1, keepdims=True)
    peak_ref[...] = jnp.broadcast_to(peak, peak_ref.shape)
    total_ref[...] = jnp.zeros_like(total_ref)
    acc_ref[...] = jnp.zeros_like(acc_ref)

    @pl.loop(0, blocks)
    def _(b):
        at = pl.multiple_of(b * block, block)
        weights = jnp.exp(scores_ref[b] - jnp.tile(peak_ref[...], (1, block // 128)))
        total_ref[...] += over_lanes(jnp.add, weights)
        acc_ref[...] += jnp.dot(
            weights.astype(jnp.bfloat16),
            values_ref[0, pl.ds(at, block), :],
            preferred_element_type=jnp.float32,
        )

    total = jnp.sum(total_ref[...], axis=1, keepdims=True)
    prefix_normed = (acc_ref[...] / total).astype(jnp.bfloat16)
    prefix_lse = peak_ref[...][:, :1] + jnp.log(total)

    own = lax.dot_general(
        q_ref[0], own_keys, dims, preferred_element_type=jnp.float32
    ) * scale
    token = lax.rem(lax.broadcasted_iota(jnp.int32, (rows, SL), 0), SL)
    other = lax.broadcasted_iota(jnp.int32, (rows, SL), 1)
    own = jnp.where(other <= token, own, MASKED)
    own_peak = jnp.max(own, axis=1, keepdims=True)
    own_weights = jnp.exp(own - own_peak)
    own_total = jnp.sum(own_weights, axis=1, keepdims=True)
    own_out = jnp.dot(
        own_weights.astype(jnp.bfloat16), own_values, preferred_element_type=jnp.float32
    )
    top = jnp.maximum(prefix_lse, own_peak)
    first = jnp.exp(prefix_lse - top)
    second = jnp.exp(own_peak - top)
    divisor = first + own_total * second
    mixed = (prefix_normed.astype(jnp.float32) * first + own_out * second) / divisor
    mixed = mixed.astype(jnp.bfloat16)
    for h in range(group):
        out_ref[:, h * HD : (h + 1) * HD] = mixed[h * SL : (h + 1) * SL, :]


def attend(docs, lengths, queries, own_keys, own_values, keys, values):
    suffixes, rows, _ = queries.shape
    length = keys.shape[1]
    wide = rows // SL * HD
    block = pl.BlockSpec
    mine = lambda i, doc, size: (i, 0, 0)
    cached = lambda i, doc, size: (doc[i], 0, 0)
    flops = 4 * suffixes * rows * length * HD
    return pl.pallas_call(
        attend_kernel,
        out_shape=jax.ShapeDtypeStruct((suffixes * SL, wide), jnp.bfloat16),
        grid_spec=pltpu.PrefetchScalarGridSpec(
            num_scalar_prefetch=2,
            grid=(suffixes,),
            in_specs=[
                block((1, rows, HD), mine),
                block((1, SL, HD), mine),
                block((1, SL, HD), mine),
                block((1, length, HD), cached),
                block((1, length, HD), cached),
            ],
            out_specs=block((SL, wide), lambda i, doc, size: (i, 0)),
            scratch_shapes=[
                pltpu.VMEM((length // KEY_BLOCK, rows, KEY_BLOCK), jnp.float32),
                pltpu.VMEM((rows, 128), jnp.float32),
                pltpu.VMEM((rows, 128), jnp.float32),
                pltpu.VMEM((rows, HD), jnp.float32),
            ],
        ),
        compiler_params=pltpu.CompilerParams(
            dimension_semantics=("arbitrary",), vmem_limit_bytes=40 << 20
        ),
        cost_estimate=pl.CostEstimate(
            flops=flops, transcendentals=flops // (4 * HD), bytes_accessed=16 << 20
        ),
    )(docs, lengths, queries, own_keys, own_values, keys, values)


def place():
    c = lax.axis_index("corpus")
    f = lax.axis_index("fsdp")
    return c, lax.div(f, 2), lax.rem(f, 2)


def flip(value, bits):
    low, high = lax.rem(value, 2), lax.div(value, 2)
    if bits & 1:
        low = 1 - low
    if bits & 2:
        high = 1 - high
    return 2 * high + low


def remote(src, dst, send, recv, c, z, k):
    return pltpu.make_async_remote_copy(
        src_ref=src,
        dst_ref=dst,
        send_sem=send,
        recv_sem=recv,
        device_id=(c, 2 * z + k),
        device_id_type=MESH,
    )


def greet(peers):
    barrier = pltpu.get_barrier_semaphore()
    for c, z, k in peers:
        pl.semaphore_signal(barrier, inc=1, device_id=(c, 2 * z + k), device_id_type=MESH)
    pl.semaphore_wait(barrier, len(peers))


def move_kernel(
    x_ref,
    wq_ref,
    wk_ref,
    wv_ref,
    kc_ref,
    vc_ref,
    facts_ref,
    gain_ref,
    qb_ref,
    kb_ref,
    vb_ref,
    ct_ref,
    st_ref,
    q_ref,
    ok_ref,
    ov_ref,
    facts_out,
    keys_ref,
    values_ref,
    acts,
    wbuf,
    normed,
    acc,
    cos_ref,
    sin_ref,
    zs,
    zr,
    xs,
    xr,
    ms,
    mr,
    ws,
    wr,
    wcs,
    wcr,
    kds,
    kr,
    kps,
    kfs,
    kcs,
    kcr,
    local,
):
    c, z, k = place()
    head = lax.div(z, 2)
    f = 2 * z + k
    inner = jnp.logical_or(z == 1, z == 2)
    greet(
        [(c, flip(z, s), k) for s in (1, 2, 3)]
        + [(flip(c, p), z, k) for p in (1, 2, 3)]
        + [(c, z, 1 - k)]
    )
    caches = (kc_ref, vc_ref)
    kept = (keys_ref, values_ref)

    def act_up(j, src):
        return remote(src, acts.at[j, c], zs.at[0, j], zr.at[j], c, lax.rem(z + 1, LINES), k)

    def act_down(j, src):
        return remote(src, acts.at[j, c], zs.at[1, j], zr.at[j], c, lax.rem(z + LINES - 1, LINES), k)

    def act_side(j, p, src):
        return remote(src, acts.at[j, c], xs.at[j, p - 1], xr.at[j, p - 1], flip(c, p), z, k)

    def fact_to(s):
        return remote(facts_ref, facts_out.at[z], ms.at[s - 1], mr.at[s - 1], c, flip(z, s), k)

    def weight_to(s):
        to = flip(z, s)
        slot = wbuf.at[f]
        at = pl.multiple_of(to * (4 * HD), 4 * HD)
        kv = pl.multiple_of(lax.div(to, 2) * HD, HD)
        parts = (
            (wq_ref.at[:, pl.ds(at, 4 * HD)], slot.at[:, 0 : 4 * HD]),
            (wk_ref.at[:, pl.ds(kv, HD)], slot.at[:, 4 * HD : 5 * HD]),
            (wv_ref.at[:, pl.ds(kv, HD)], slot.at[:, 5 * HD : 6 * HD]),
        )
        if s == 0:
            return [pltpu.make_async_copy(a, b, local.at[i]) for i, (a, b) in enumerate(parts)]
        return [
            remote(a, b, ws.at[s - 1, i], wr.at[s - 1, i], c, to, k)
            for i, (a, b) in enumerate(parts)
        ]

    def weight_core(s):
        slot = wbuf.at[2 * flip(z, s) + k]
        return remote(slot, slot, wcs.at[s], wcr.at[s], c, z, 1 - k)

    def own_slice(t, which):
        at = pl.multiple_of(which * HD, HD)
        return caches[t].at[0, :, pl.ds(at, HD)]

    def kv_partner(t):
        return remote(own_slice(t, head), kept[t].at[f], kps.at[t], kr.at[0, t], c, flip(z, 1), k)

    def kv_across(t, s):
        return remote(
            own_slice(t, 1 - head), kept[t].at[f], kds.at[t], kr.at[s - 1, t], c, flip(z, s), k
        )

    def kv_forward(t, s):
        slot = kept[t].at[2 * flip(z, s) + k]
        return remote(slot, slot, kfs.at[s - 2, t], kr.at[(s ^ 1) - 1, t], c, flip(z, 1), k)

    def kv_core(t, s):
        slot = kept[t].at[2 * flip(z, s) + k]
        src = own_slice(t, head) if s == 0 else slot
        return remote(src, slot, kcs.at[s, t], kcr.at[s, t], c, z, 1 - k)

    def kv_local(t):
        return pltpu.make_async_copy(own_slice(t, head), kept[t].at[f], local.at[3 + t])

    act_own = pltpu.make_async_copy(x_ref, acts.at[z, c], local.at[5])
    fact_own = pltpu.make_async_copy(facts_ref, facts_out.at[z], local.at[6])

    @pl.when(z < LINES - 1)
    def _():
        act_up(z, x_ref).start()

    @pl.when(z > 0)
    def _():
        act_down(z, x_ref).start()

    for s in (1, 2, 3):
        fact_to(s).start()
    for p in (1, 2, 3):
        act_side(z, p, x_ref).start()
    act_own.start()
    fact_own.start()
    for copy in weight_to(0):
        copy.start()
    for s in (1, 3, 2):
        for copy in weight_to(s):
            copy.start()

    for d in (1, 2, 3):
        @pl.when(z - d >= 0)
        def _():
            j = z - d
            block = acts.at[j, c]
            act_up(j, block).wait_recv()

            @pl.when(z < LINES - 1)
            def _():
                act_up(j, block).start()

            for p in (1, 2, 3):
                act_side(j, p, block).start()

        @pl.when(z + d < LINES)
        def _():
            j = z + d
            block = acts.at[j, c]
            act_down(j, block).wait_recv()

            @pl.when(z > 0)
            def _():
                act_down(j, block).start()

            for p in (1, 2, 3):
                act_side(j, p, block).start()

    for copy in weight_to(0):
        copy.wait()
    weight_core(0).start()
    for s in (1, 3, 2):
        for copy in weight_to(s):
            copy.wait_recv()
        weight_core(s).start()

    for t in (0, 1):
        kv_partner(t).start()
    for t in (0, 1):
        @pl.when(inner)
        def _():
            kv_across(t, 3).start()

        @pl.when(jnp.logical_not(inner))
        def _():
            kv_across(t, 2).start()
    for t in (0, 1):
        kv_local(t).start()
        kv_core(t, 0).start()

    for s in range(4):
        weight_core(s).wait_recv()
    for s in (1, 2, 3):
        fact_to(s).wait_recv()
    fact_own.wait()
    act_own.wait()

    def project(j):
        for p in (1, 2, 3):
            act_side(j, p, acts.at[j, c]).wait_recv()

        @pl.loop(0, 4)
        def _(r):
            at = pl.multiple_of(r * SL, SL)
            total = jnp.zeros((SL, 1), jnp.float32)
            for i in range(COLUMNS):
                wide = acts[j, i, pl.ds(at, SL), :].astype(jnp.float32)
                total += jnp.sum(wide * wide, axis=1, keepdims=True)
            inv = lax.rsqrt(total / (COLUMNS * acts.shape[3]) + EPS)
            for i in range(COLUMNS):
                wide = acts[j, i, pl.ds(at, SL), :].astype(jnp.float32)
                columns = pl.ds(i * acts.shape[3], acts.shape[3])
                normed[pl.ds(at, SL), columns] = (wide * inv * gain_ref[:, columns]).astype(jnp.bfloat16)
            cosl = facts_out[j, pl.ds(r, 1), :]
            sinl = facts_out[j, pl.ds(r + 4, 1), :]
            cos_ref[pl.ds(at, SL), :] = cosl * ct_ref[...] - sinl * st_ref[...]
            sin_ref[pl.ds(at, SL), :] = sinl * ct_ref[...] + cosl * st_ref[...]

        acc[...] = jnp.zeros_like(acc)
        depth = wbuf.shape[1]

        @pl.loop(0, 2 * LINES)
        def _(i):
            at = pl.multiple_of(i * depth, depth)
            acc[...] += jnp.dot(normed[:, pl.ds(at, depth)], wbuf[i], preferred_element_type=jnp.float32)

        cosine, sine = cos_ref[...], sin_ref[...]
        for h in range(4):
            lin = acc[:, h * HD : (h + 1) * HD] + qb_ref[pl.ds(4 * z + h, 1), :]
            turned = rotate(lin, cosine, sine).astype(jnp.bfloat16)
            for i in range(4):
                q_ref[4 * j + i, h * SL : (h + 1) * SL, :] = turned[i * SL : (i + 1) * SL]
        lin = acc[:, 4 * HD : 5 * HD] + kb_ref[pl.ds(head, 1), :]
        turned = rotate(lin, cosine, sine).astype(jnp.bfloat16)
        straight = (acc[:, 5 * HD : 6 * HD] + vb_ref[pl.ds(head, 1), :]).astype(jnp.bfloat16)
        for i in range(4):
            ok_ref[4 * j + i] = turned[i * SL : (i + 1) * SL]
            ov_ref[4 * j + i] = straight[i * SL : (i + 1) * SL]

    @pl.loop(0, LINES)
    def _(j):
        project(j)

    for t in (0, 1):
        kv_partner(t).wait_recv()
        kv_core(t, 1).start()

    @pl.when(inner)
    def _():
        for s in (3, 2):
            for t in (0, 1):
                kv_across(t, s).wait_recv()
                kv_forward(t, s).start()
                kv_core(t, s).start()

    @pl.when(jnp.logical_not(inner))
    def _():
        for s in (2, 3):
            for t in (0, 1):
                kv_across(t, s).wait_recv()
                kv_core(t, s).start()

    for j in range(LINES):
        for p in (1, 2, 3):
            act_side(j, p, acts.at[j, c]).wait_send()

        @pl.when(jnp.logical_and(z < LINES - 1, j <= z))
        def _():
            act_up(j, acts.at[j, c]).wait_send()

        @pl.when(jnp.logical_and(z > 0, j >= z))
        def _():
            act_down(j, acts.at[j, c]).wait_send()

    for s in (1, 2, 3):
        fact_to(s).wait_send()
        for copy in weight_to(s):
            copy.wait_send()
    for s in range(4):
        weight_core(s).wait_send()
    for t in (0, 1):
        kv_partner(t).wait_send()
        kv_across(t, 2).wait_send()
        kv_local(t).wait()

        @pl.when(inner)
        def _():
            for s in (2, 3):
                kv_forward(t, s).wait_send()

        for s in range(4):
            kv_core(t, s).wait()


def move(inputs, w_query, w_key, w_value, key_cache, value_cache, facts, gain, q_bias, k_bias, v_bias, ct, st):
    tokens, wide = inputs.shape
    depth = w_query.shape[0]
    length = key_cache.shape[1]
    docs = 2 * LINES
    own = tokens // SL
    held = pl.BlockSpec(memory_space=pltpu.VMEM)
    far = pl.BlockSpec(memory_space=pl.ANY)
    dma = pltpu.SemaphoreType.DMA
    bf16 = jnp.bfloat16
    flops = 2 * LINES * tokens * wide * COLUMNS * 6 * HD
    return pl.pallas_call(
        move_kernel,
        out_shape=(
            jax.ShapeDtypeStruct((LINES * own, 4 * SL, HD), bf16),
            jax.ShapeDtypeStruct((LINES * own, SL, HD), bf16),
            jax.ShapeDtypeStruct((LINES * own, SL, HD), bf16),
            jax.ShapeDtypeStruct((LINES,) + facts.shape, jnp.float32),
            jax.ShapeDtypeStruct((docs, length, HD), bf16),
            jax.ShapeDtypeStruct((docs, length, HD), bf16),
        ),
        in_specs=[far] * 6 + [held] * 7,
        out_specs=(held, held, held, held, far, far),
        scratch_shapes=[
            pltpu.VMEM((LINES, COLUMNS, tokens, wide), bf16),
            pltpu.VMEM((docs, depth, 6 * HD), bf16),
            pltpu.VMEM((tokens, wide * COLUMNS), bf16),
            pltpu.VMEM((tokens, 6 * HD), jnp.float32),
            pltpu.VMEM((tokens, HD), jnp.float32),
            pltpu.VMEM((tokens, HD), jnp.float32),
            dma((2, LINES)),
            dma((LINES,)),
            dma((LINES, 3)),
            dma((LINES, 3)),
            dma((3,)),
            dma((3,)),
            dma((3, 3)),
            dma((3, 3)),
            dma((4,)),
            dma((4,)),
            dma((2,)),
            dma((3, 2)),
            dma((2,)),
            dma((2, 2)),
            dma((4, 2)),
            dma((4, 2)),
            dma((7,)),
        ],
        compiler_params=pltpu.CompilerParams(
            collective_id=0, has_side_effects=True, vmem_limit_bytes=48 << 20
        ),
        cost_estimate=pl.CostEstimate(flops=flops, transcendentals=0, bytes_accessed=32 << 20),
    )(inputs, w_query, w_key, w_value, key_cache, value_cache, facts, gain, q_bias, k_bias, v_bias, ct, st)


def return_kernel(a_ref, out_ref, send, recv, local):
    c, z, k = place()
    tokens = out_ref.shape[0]
    wide = a_ref.shape[1]
    greet([(c, flip(z, s), k) for s in (1, 2, 3)])
    columns = pl.ds(pl.multiple_of(z * wide, wide), wide)

    def rows(to):
        return a_ref.at[pl.ds(pl.multiple_of(to * tokens, tokens), tokens), :]

    def send_to(s):
        to = flip(z, s)
        return remote(rows(to), out_ref.at[:, columns], send.at[s - 1], recv.at[s - 1], c, to, k)

    own = pltpu.make_async_copy(rows(z), out_ref.at[:, columns], local.at[0])
    for s in (2, 3, 1):
        send_to(s).start()
    own.start()
    own.wait()
    for s in (1, 2, 3):
        send_to(s).wait()


def give_back(array):
    tokens = array.shape[0] // LINES
    wide = array.shape[1]
    far = pl.BlockSpec(memory_space=pl.ANY)
    dma = pltpu.SemaphoreType.DMA
    return pl.pallas_call(
        return_kernel,
        out_shape=jax.ShapeDtypeStruct((tokens, wide * LINES), jnp.bfloat16),
        in_specs=[far],
        out_specs=far,
        scratch_shapes=[dma((3,)), dma((3,)), dma((1,))],
        compiler_params=pltpu.CompilerParams(collective_id=1, has_side_effects=True),
        cost_estimate=pl.CostEstimate(flops=0, transcendentals=0, bytes_accessed=2 << 20),
    )(array)


def heads_by_line(
    inputs,
    norm_gain,
    w_query,
    w_key,
    w_value,
    query_bias,
    key_bias,
    value_bias,
    key_cache,
    value_cache,
    source_doc,
    prefix_len,
):
    start_cos, start_sin = rope_tables(prefix_len, HD)
    step_cos, step_sin = rope_tables(jnp.arange(SL, dtype=jnp.int32), HD)
    own = prefix_len.shape[0]
    numbers = jnp.stack([source_doc, prefix_len]).astype(jnp.float32)
    numbers = jnp.pad(numbers, ((0, 8 - numbers.shape[0]), (0, 128 - own)))
    facts = jnp.concatenate([start_cos, start_sin, numbers])
    queries, own_keys, own_values, facts, keys, values = move(
        inputs,
        w_query,
        w_key,
        w_value,
        key_cache,
        value_cache,
        facts,
        norm_gain[None],
        query_bias.reshape(-1, HD),
        key_bias.reshape(-1, HD),
        value_bias.reshape(-1, HD),
        step_cos,
        step_sin,
    )
    numbers = facts[:, 2 * own : 2 * own + 2, :own].astype(jnp.int32)
    docs, lengths = numbers[:, 0].reshape(-1), numbers[:, 1].reshape(-1)
    out = attend(docs, lengths, queries, own_keys, own_values, keys, values)
    return give_back(out)


def dense_attend(source_doc, prefix_len, q_lin, k_lin, v_lin, cosine, sine, keys, values):
    suffixes = source_doc.shape[0]
    kv_heads = k_lin.shape[1] // HD
    group = q_lin.shape[1] // k_lin.shape[1]

    def turned(lin):
        vector = lin.reshape(suffixes * SL, -1, HD)
        other = jnp.roll(vector, HD // 2, axis=-1)
        return (vector * cosine[:, None] + other * sine[:, None]).astype(jnp.bfloat16)

    queries = turned(q_lin).reshape(suffixes, SL, kv_heads, group, HD)
    queries = queries.transpose(0, 2, 3, 1, 4).reshape(suffixes * kv_heads, group * SL, HD)
    own_keys = turned(k_lin).reshape(suffixes, SL, kv_heads, HD).swapaxes(1, 2).reshape(-1, SL, HD)
    own_values = v_lin.astype(jnp.bfloat16)
    own_values = own_values.reshape(suffixes, SL, kv_heads, HD).swapaxes(1, 2).reshape(-1, SL, HD)

    def by_head(cache):
        return cache.reshape(-1, cache.shape[1], kv_heads, HD).swapaxes(1, 2).reshape(-1, cache.shape[1], HD)

    docs = (source_doc[:, None] * kv_heads + jnp.arange(kv_heads, dtype=jnp.int32)[None, :]).reshape(-1)
    lengths = jnp.repeat(prefix_len, kv_heads)
    out = attend(docs, lengths, queries, own_keys, own_values, by_head(keys), by_head(values))
    out = out.reshape(suffixes, kv_heads, SL, group * HD).swapaxes(1, 2)
    return out.reshape(suffixes * SL, kv_heads * group * HD)


def gather_all(
    inputs,
    norm_gain,
    w_query,
    w_key,
    w_value,
    query_bias,
    key_bias,
    value_bias,
    key_cache,
    value_cache,
    source_doc,
    prefix_len,
):
    full_rows = lax.all_gather(inputs, "corpus", axis=1, tiled=True)
    normed = normalize(full_rows, norm_gain)

    def project(weight, bias):
        whole = lax.all_gather(weight, "fsdp", axis=0, tiled=True)
        return jnp.dot(normed, whole, preferred_element_type=jnp.float32) + bias

    q_lin, k_lin, v_lin = project(w_query, query_bias), project(w_key, key_bias), project(w_value, value_bias)
    keys = lax.all_gather(key_cache, "fsdp", axis=0, tiled=True)
    values = lax.all_gather(value_cache, "fsdp", axis=0, tiled=True)
    position = prefix_len[:, None] + jnp.arange(SL, dtype=jnp.int32)[None, :]
    cosine, sine = rope_tables(position.reshape(-1), HD)
    return dense_attend(source_doc, prefix_len, q_lin, k_lin, v_lin, cosine, sine, keys, values)


def shards(*arrays):
    fits = (
        lax.axis_size("fsdp") == 2 * LINES
        and lax.axis_size("corpus") == COLUMNS
        and arrays[2].shape[1] == LINES * 4 * HD
        and arrays[3].shape[1] == 2 * HD
    )
    return heads_by_line(*arrays) if fits else gather_all(*arrays)


def solution(mesh):
    in_specs = (
        P("fsdp", "corpus"),
        P(),
        P("fsdp", "corpus"),
        P("fsdp", "corpus"),
        P("fsdp", "corpus"),
        P("corpus"),
        P("corpus"),
        P("corpus"),
        P("fsdp", None, "corpus"),
        P("fsdp", None, "corpus"),
        P("fsdp"),
        P("fsdp"),
    )
    out_specs = P("fsdp", "corpus")
    return jax.shard_map(shards, mesh=mesh, in_specs=in_specs, out_specs=out_specs, check_vma=False)
```

```python
import functools

import jax
import jax.numpy as jnp
from jax import lax
from jax.experimental import pallas as pl
from jax.experimental.pallas import tpu as pltpu
from jax.sharding import PartitionSpec as P

HD = 128
SL = 64
EPS = 1e-06
THETA = 1000000.0
MASKED = -1e30
KEY_BLOCK = 512
ROW_BLOCK = 256
MESH = pl.DeviceIdType.MESH
LINES = 4
COLUMNS = 4


def rope_tables(position, width):
    half = width // 2
    freq = THETA ** (-(jnp.arange(half, dtype=jnp.float32) * 2.0 / width))
    angle = position.astype(jnp.float32)[..., None] * freq
    cosine, sine = jnp.cos(angle), jnp.sin(angle)
    return (
        jnp.concatenate([cosine, cosine], axis=-1),
        jnp.concatenate([-sine, sine], axis=-1),
    )


def normalize(rows, norm_gain):
    wide = rows.astype(jnp.float32)
    spread = jnp.mean(wide * wide, axis=-1, keepdims=True)
    return (wide * lax.rsqrt(spread + EPS) * norm_gain).astype(jnp.bfloat16)


def rotate(vector, cosine, sine):
    return vector * cosine + pltpu.roll(vector, HD // 2, 1) * sine


def over_lanes(op, array):
    parts = [array[:, at : at + 128] for at in range(0, array.shape[1], 128)]
    while len(parts) > 1:
        parts = [op(a, b) for a, b in zip(parts[::2], parts[1::2])]
    return parts[0]


def attend_kernel(
    first,
    row_ref,
    doc_ref,
    len_ref,
    q_ref,
    k_ref,
    v_ref,
    keys_ref,
    values_ref,
    out_ref,
    peak_ref,
    total_ref,
    acc_ref,
):
    length = len_ref[first + pl.program_id(0)]
    scale = HD ** (-0.5)
    rows = q_ref.shape[1]
    group = rows // SL
    dims = (((1,), (1,)), ((), ()))
    block = KEY_BLOCK
    most = keys_ref.shape[1] // block
    blocks = lax.div(length + (block - 1), block)

    def prefix(count):
        for at in range(0, rows, ROW_BLOCK):
            part = slice(at, at + ROW_BLOCK)
            scores = []
            for b in range(count):
                score = lax.dot_general(
                    q_ref[0, part, :],
                    keys_ref[0, b * block : (b + 1) * block, :],
                    dims,
                    preferred_element_type=jnp.float32,
                )
                if b == count - 1:
                    column = lax.broadcasted_iota(jnp.int32, (1, block), 1) + b * block
                    score = jnp.where(column < length, score, MASKED)
                scores.append(score)
            peak = functools.reduce(jnp.maximum, [over_lanes(jnp.maximum, s) for s in scores])
            peak = jnp.broadcast_to(jnp.max(peak, axis=1, keepdims=True), peak.shape)
            peak_ref[part, :] = peak
            total, acc = 0.0, 0.0
            for b in range(count):
                weights = jnp.exp((scores[b] - jnp.tile(peak, (1, block // 128))) * scale)
                total += over_lanes(jnp.add, weights)
                acc += jnp.dot(
                    weights.astype(jnp.bfloat16),
                    values_ref[0, b * block : (b + 1) * block, :],
                    preferred_element_type=jnp.float32,
                )
            total_ref[part, :] = total
            acc_ref[part, :] = acc

    for count in range(1, most + 1):
        @pl.when(blocks == count)
        def _():
            prefix(count)

    @pl.when(length > 0)
    def _():
        total = jnp.sum(total_ref[...], axis=1, keepdims=True)
        prefix_normed = (acc_ref[...] / total).astype(jnp.bfloat16)
        prefix_lse = peak_ref[...][:, :1] * scale + jnp.log(total)

        own = lax.dot_general(
            q_ref[0], k_ref[0], dims, preferred_element_type=jnp.float32
        ) * scale
        token = lax.rem(lax.broadcasted_iota(jnp.int32, (rows, SL), 0), SL)
        other = lax.broadcasted_iota(jnp.int32, (rows, SL), 1)
        own = jnp.where(other <= token, own, MASKED)
        own_peak = jnp.max(own, axis=1, keepdims=True)
        own_weights = jnp.exp(own - own_peak)
        own_total = jnp.sum(own_weights, axis=1, keepdims=True)
        own_out = jnp.dot(
            own_weights.astype(jnp.bfloat16), v_ref[0], preferred_element_type=jnp.float32
        )
        top = jnp.maximum(prefix_lse, own_peak)
        former = jnp.exp(prefix_lse - top)
        latter = jnp.exp(own_peak - top)
        divisor = former + own_total * latter
        mixed = (prefix_normed.astype(jnp.float32) * former + own_out * latter) / divisor
        mixed = mixed.astype(jnp.bfloat16)
        for h in range(group):
            out_ref[:, h * HD : (h + 1) * HD] = mixed[h * SL : (h + 1) * SL, :]


def attend(row, docs, lengths, queries, own_keys, own_values, keys, values, first, count):
    rows = queries.shape[1]
    length = keys.shape[1]
    wide = rows // SL * HD
    block = pl.BlockSpec
    mine = lambda i, row, doc, size: (row[first + i], 0, 0)
    cached = lambda i, row, doc, size: (doc[first + i], 0, 0)
    flops = 2 * count * rows * length * HD
    return pl.pallas_call(
        functools.partial(attend_kernel, first),
        out_shape=jax.ShapeDtypeStruct((count * SL, wide), jnp.bfloat16),
        grid_spec=pltpu.PrefetchScalarGridSpec(
            num_scalar_prefetch=3,
            grid=(count,),
            in_specs=[
                block((1, rows, HD), mine),
                block((1, SL, HD), mine),
                block((1, SL, HD), mine),
                block((1, length, HD), cached),
                block((1, length, HD), cached),
            ],
            out_specs=block((SL, wide), lambda i, row, doc, size: (i, 0)),
            scratch_shapes=[
                pltpu.VMEM((rows, 128), jnp.float32),
                pltpu.VMEM((rows, 128), jnp.float32),
                pltpu.VMEM((rows, HD), jnp.float32),
            ],
        ),
        compiler_params=pltpu.CompilerParams(
            dimension_semantics=("arbitrary",), vmem_limit_bytes=56 << 20
        ),
        cost_estimate=pl.CostEstimate(
            flops=flops, transcendentals=flops // (4 * HD), bytes_accessed=4 << 20
        ),
    )(row, docs, lengths, queries, own_keys, own_values, keys, values)


def place():
    c = lax.axis_index("corpus")
    f = lax.axis_index("fsdp")
    return c, lax.div(f, 2), lax.rem(f, 2)


def flip(value, bits):
    low = lax.rem(lax.rem(value, 2) + bits % 2, 2)
    high = lax.rem(lax.div(value, 2) + bits // 2, 2)
    return 2 * high + low


def remote(src, dst, send, recv, c, z, k):
    return pltpu.make_async_remote_copy(
        src_ref=src,
        dst_ref=dst,
        send_sem=send,
        recv_sem=recv,
        device_id=(c, 2 * z + k),
        device_id_type=MESH,
    )


def greet(peers):
    barrier = pltpu.get_barrier_semaphore()
    for c, z, k in peers:
        pl.semaphore_signal(barrier, inc=1, device_id=(c, 2 * z + k), device_id_type=MESH)
    pl.semaphore_wait(barrier, len(peers))


def move_kernel(
    x_ref,
    wq_ref,
    wk_ref,
    wv_ref,
    kc_ref,
    vc_ref,
    facts_ref,
    gain_in,
    qb_in,
    kb_in,
    vb_in,
    ct_in,
    st_in,
    q_ref,
    ok_ref,
    ov_ref,
    facts_out,
    keys_ref,
    values_ref,
    acts,
    wbuf,
    normed,
    acc,
    cos_ref,
    sin_ref,
    facts_held,
    gain_ref,
    qb_ref,
    kb_ref,
    vb_ref,
    ct_ref,
    st_ref,
    asend,
    arecv,
    xsend,
    xrecv,
    fsend,
    frecv,
    wsend,
    wrecv,
    wcsend,
    wcrecv,
    ksend,
    krecv,
    kcsend,
    kcrecv,
    local,
):
    c, z, k = place()
    head = lax.div(z, 2)
    f = 2 * z + k
    inner = jnp.logical_or(z == 1, z == 2)
    outer = jnp.logical_not(inner)
    greet(
        [(c, flip(z, s), k) for s in (1, 2, 3)]
        + [(flip(c, p), z, k) for p in (1, 2, 3)]
        + [(c, z, 1 - k)]
    )
    group = wq_ref.shape[1] // 2
    caches = (kc_ref, vc_ref)
    kept = (keys_ref, values_ref)

    def act_to(s):
        return remote(x_ref, acts.at[z, c], asend.at[s - 1], arecv.at[s - 1], c, flip(z, s), k)

    def act_side(s, p):
        j = flip(z, s)
        src = x_ref if isinstance(s, int) and s == 0 else acts.at[j, c]
        return remote(src, acts.at[j, c], xsend.at[s, p - 1], xrecv.at[s, p - 1], flip(c, p), z, k)

    def fact_to(s):
        return remote(
            facts_ref, facts_held.at[z], fsend.at[s - 1], frecv.at[s - 1], c, flip(z, s), k
        )

    def weight_to(s, which_parts=(0, 1, 2)):
        to = flip(z, s)
        slot = wbuf.at[f]
        which = lax.div(to, 2)
        at = pl.multiple_of(which * group, group)
        kv = pl.multiple_of(which * HD, HD)
        parts = (
            (wk_ref.at[:, pl.ds(kv, HD)], slot.at[:, group : group + HD]),
            (wv_ref.at[:, pl.ds(kv, HD)], slot.at[:, group + HD : group + 2 * HD]),
            (wq_ref.at[:, pl.ds(at, group)], slot.at[:, 0:group]),
        )
        if s == 0:
            return [pltpu.make_async_copy(*parts[i], local.at[i]) for i in which_parts]
        return [
            remote(*parts[i], wsend.at[s - 1, i], wrecv.at[s - 1, i], c, to, k) for i in which_parts
        ]

    def weight_core(s):
        slot = wbuf.at[2 * flip(z, s) + k]
        return remote(slot, slot, wcsend.at[s], wcrecv.at[s], c, z, 1 - k)

    def own_slice(t, which):
        at = pl.multiple_of(which * HD, HD)
        return caches[t].at[0, :, pl.ds(at, HD)]

    def kv_to(s, t):
        to = flip(z, s)
        return remote(
            own_slice(t, lax.div(to, 2)), kept[t].at[f], ksend.at[s - 1, t], krecv.at[s - 1, t], c, to, k
        )

    def kv_core(s, t):
        slot = kept[t].at[2 * flip(z, s) + k]
        src = own_slice(t, head) if s == 0 else slot
        return remote(src, slot, kcsend.at[s, t], kcrecv.at[s, t], c, z, 1 - k)

    def kv_local(t):
        return pltpu.make_async_copy(own_slice(t, head), kept[t].at[f], local.at[3 + t])

    act_own = pltpu.make_async_copy(x_ref, acts.at[z, c], local.at[5])
    fact_own = pltpu.make_async_copy(facts_ref, facts_held.at[z], local.at[6])
    small = [
        pltpu.make_async_copy(a, b, local.at[7 + i])
        for i, (a, b) in enumerate(
            (
                (gain_in, gain_ref),
                (qb_in, qb_ref),
                (kb_in, kb_ref),
                (vb_in, vb_ref),
                (ct_in, ct_ref),
                (st_in, st_ref),
            )
        )
    ]

    def project(s):
        j = flip(z, s)
        for p in (1, 2, 3):
            act_side(s, p).wait_recv()

        @pl.loop(0, 4)
        def _(r):
            at = pl.multiple_of(r * SL, SL)
            total = jnp.zeros((SL, 1), jnp.float32)
            for i in range(COLUMNS):
                wide = acts[j, i, pl.ds(at, SL), :].astype(jnp.float32)
                total += jnp.sum(wide * wide, axis=1, keepdims=True)
            inv = lax.rsqrt(total / (COLUMNS * acts.shape[3]) + EPS)
            for i in range(COLUMNS):
                wide = acts[j, i, pl.ds(at, SL), :].astype(jnp.float32)
                columns = pl.ds(i * acts.shape[3], acts.shape[3])
                normed[pl.ds(at, SL), columns] = (wide * inv * gain_ref[:, columns]).astype(jnp.bfloat16)
            cosl = facts_held[j, pl.ds(r, 1), :]
            sinl = facts_held[j, pl.ds(r + 4, 1), :]
            cos_ref[pl.ds(at, SL), :] = cosl * ct_ref[...] - sinl * st_ref[...]
            sin_ref[pl.ds(at, SL), :] = sinl * ct_ref[...] + cosl * st_ref[...]

        acc[...] = jnp.zeros_like(acc)
        depth = wbuf.shape[1]

        @pl.loop(0, 2 * LINES)
        def _(i):
            at = pl.multiple_of(i * depth, depth)
            acc[...] += jnp.dot(normed[:, pl.ds(at, depth)], wbuf[i], preferred_element_type=jnp.float32)

        cosine, sine = cos_ref[...], sin_ref[...]
        heads = group // HD
        for h in range(heads):
            lin = acc[:, h * HD : (h + 1) * HD] + qb_ref[pl.ds(heads * head + h, 1), :]
            turned = rotate(lin, cosine, sine).astype(jnp.bfloat16)
            for i in range(4):
                q_ref[4 * j + i, h * SL : (h + 1) * SL, :] = turned[i * SL : (i + 1) * SL]
        lin = acc[:, group : group + HD] + kb_ref[pl.ds(head, 1), :]
        turned = rotate(lin, cosine, sine).astype(jnp.bfloat16)
        straight = (acc[:, group + HD : group + 2 * HD] + vb_ref[pl.ds(head, 1), :]).astype(jnp.bfloat16)
        for i in range(4):
            ok_ref[4 * j + i] = turned[i * SL : (i + 1) * SL]
            ov_ref[4 * j + i] = straight[i * SL : (i + 1) * SL]

    @pl.when(outer)
    def _():
        for s in (2, 1):
            act_to(s).start()
        for s in (1, 2, 3):
            fact_to(s).start()
        fact_own.start()
        for s in (2, 1):
            for copy in weight_to(s, (0, 1)):
                copy.start()
        for s in (2, 1):
            act_to(s).wait_send()
            weight_to(s, (2,))[0].start()
        for s in (2, 1):
            weight_to(s, (2,))[0].wait_send()
            for t in (0, 1):
                kv_to(s, t).start()
        for s in (1, 2, 3):
            fact_to(s).wait()
        fact_own.wait()
        facts_out[...] = facts_held[...]
        for s in (2, 1):
            for copy in weight_to(s, (0, 1)):
                copy.wait_send()
            for t in (0, 1):
                kv_to(s, t).wait_send()

    @pl.when(inner)
    def _():
        act_to(3).start()
        for s in (1, 2, 3):
            fact_to(s).start()
        fact_own.start()
        for p in (1, 2, 3):
            act_side(0, p).start()
        act_own.start()
        for copy in weight_to(0):
            copy.start()
        for copy in weight_to(3, (0, 1)):
            copy.start()
        for copy in small:
            copy.start()
        for t in (0, 1):
            kv_local(t).start()
            kv_core(0, t).start()
        act_to(3).wait_send()
        weight_to(3, (2,))[0].start()
        for s in (1, 3, 2):
            act_to(s).wait_recv()
            for p in (1, 2, 3):
                act_side(s, p).start()
        for copy in weight_to(0):
            copy.wait()
        weight_core(0).start()
        for s in (1, 3):
            for copy in weight_to(s):
                copy.wait_recv()
            weight_core(s).start()
        for copy in weight_to(3):
            copy.wait_send()
        for t in (0, 1):
            kv_to(3, t).start()
        for copy in weight_to(2):
            copy.wait_recv()
        weight_core(2).start()

        for s in (1, 2, 3):
            fact_to(s).wait()
        fact_own.wait()
        facts_out[...] = facts_held[...]
        act_own.wait()
        for copy in small:
            copy.wait()
        for s in range(4):
            weight_core(s).wait_recv()

        @pl.loop(0, LINES)
        def _(i):
            project(jnp.where(i < 2, i, 5 - i))

        for t in (0, 1):
            for s in (1, 3, 2):
                kv_to(s, t).wait_recv()
                kv_core(s, t).start()

        act_sides = [act_side(s, p) for s in range(4) for p in (1, 2, 3)]
        for copy in act_sides:
            copy.wait_send()
        for s in range(4):
            weight_core(s).wait_send()
        for t in (0, 1):
            kv_to(3, t).wait_send()
            kv_local(t).wait()
            for s in range(4):
                kv_core(s, t).wait()


def move(inputs, w_query, w_key, w_value, key_cache, value_cache, facts, *small):
    tokens, wide = inputs.shape
    depth = w_query.shape[0]
    group = w_query.shape[1] // 2
    length = key_cache.shape[1]
    docs = 2 * LINES
    suffixes = LINES * (tokens // SL)
    held = pl.BlockSpec(memory_space=pltpu.VMEM)
    far = pl.BlockSpec(memory_space=pltpu.HBM)
    dma = pltpu.SemaphoreType.DMA
    bf16, f32 = jnp.bfloat16, jnp.float32
    flops = 2 * LINES * tokens * wide * COLUMNS * (group + 2 * HD)
    return pl.pallas_call(
        move_kernel,
        out_shape=(
            jax.ShapeDtypeStruct((suffixes, group // HD * SL, HD), bf16),
            jax.ShapeDtypeStruct((suffixes, SL, HD), bf16),
            jax.ShapeDtypeStruct((suffixes, SL, HD), bf16),
            jax.ShapeDtypeStruct((LINES,) + facts.shape, f32),
            jax.ShapeDtypeStruct((docs, length, HD), bf16),
            jax.ShapeDtypeStruct((docs, length, HD), bf16),
        ),
        in_specs=[far] * 13,
        out_specs=(held, held, held, held, far, far),
        scratch_shapes=[
            pltpu.VMEM((LINES, COLUMNS, tokens, wide), bf16),
            pltpu.VMEM((docs, depth, group + 2 * HD), bf16),
            pltpu.VMEM((tokens, wide * COLUMNS), bf16),
            pltpu.VMEM((tokens, group + 2 * HD), f32),
            pltpu.VMEM((tokens, HD), f32),
            pltpu.VMEM((tokens, HD), f32),
            pltpu.VMEM((LINES,) + facts.shape, f32),
            *[pltpu.VMEM(array.shape, f32) for array in small],
            dma((3,)),
            dma((3,)),
            dma((4, 3)),
            dma((4, 3)),
            dma((3,)),
            dma((3,)),
            dma((3, 3)),
            dma((3, 3)),
            dma((4,)),
            dma((4,)),
            dma((3, 2)),
            dma((3, 2)),
            dma((4, 2)),
            dma((4, 2)),
            dma((13,)),
        ],
        compiler_params=pltpu.CompilerParams(
            collective_id=0, has_side_effects=True, vmem_limit_bytes=56 << 20
        ),
        cost_estimate=pl.CostEstimate(flops=flops, transcendentals=0, bytes_accessed=32 << 20),
    )(inputs, w_query, w_key, w_value, key_cache, value_cache, facts, *small)


def heads_by_line(
    inputs,
    norm_gain,
    w_query,
    w_key,
    w_value,
    query_bias,
    key_bias,
    value_bias,
    key_cache,
    value_cache,
    source_doc,
    prefix_len,
):
    c, z, k = place()
    inner = jnp.logical_or(z == 1, z == 2)
    head = lax.div(z, 2)
    start_cos, start_sin = rope_tables(prefix_len, HD)
    step_cos, step_sin = rope_tables(jnp.arange(SL, dtype=jnp.int32), HD)
    own = prefix_len.shape[0]
    numbers = jnp.stack([source_doc, prefix_len]).astype(jnp.float32)
    numbers = jnp.pad(numbers, ((0, 8 - numbers.shape[0]), (0, 128 - own)))
    facts = jnp.concatenate([start_cos, start_sin, numbers])
    queries, own_keys, own_values, facts, keys, values = move(
        inputs,
        w_query,
        w_key,
        w_value,
        key_cache,
        value_cache,
        facts,
        norm_gain[None],
        query_bias.reshape(-1, HD),
        key_bias.reshape(-1, HD),
        value_bias.reshape(-1, HD),
        step_cos,
        step_sin,
    )
    order = (2, 3, 1, 0)
    row = jnp.concatenate([own * flip(z, s) + jnp.arange(own, dtype=jnp.int32) for s in order])
    numbers = facts[:, 2 * own : 2 * own + 2, :own].astype(jnp.int32)
    docs, lengths = numbers[:, 0].reshape(-1)[row], numbers[:, 1].reshape(-1)[row]
    docs = jnp.where(inner, docs, 0)
    lengths = jnp.where(inner, lengths, 0)
    row = jnp.where(inner, row, 0)
    outs = {}
    for at, s in enumerate(order):
        out = attend(row, docs, lengths, queries, own_keys, own_values, keys, values, own * at, own)
        if s:
            pairs = [(2 * a + b, 2 * (a ^ s) + b) for a in (1, 2) for b in (0, 1)]
            out = lax.ppermute(out, "fsdp", pairs)
        outs[s] = out
    same = jnp.where(inner, outs[0], outs[1])
    other = jnp.where(inner, outs[3], outs[2])
    return jnp.where(
        head == 0,
        jnp.concatenate([same, other], axis=1),
        jnp.concatenate([other, same], axis=1),
    )


def dense_attend(source_doc, prefix_len, q_lin, k_lin, v_lin, cosine, sine, keys, values):
    suffixes = source_doc.shape[0]
    kv_heads = k_lin.shape[1] // HD
    group = q_lin.shape[1] // k_lin.shape[1]

    def turned(lin):
        vector = lin.reshape(suffixes * SL, -1, HD)
        other = jnp.roll(vector, HD // 2, axis=-1)
        return (vector * cosine[:, None] + other * sine[:, None]).astype(jnp.bfloat16)

    queries = turned(q_lin).reshape(suffixes, SL, kv_heads, group, HD)
    queries = queries.transpose(0, 2, 3, 1, 4).reshape(suffixes * kv_heads, group * SL, HD)
    own_keys = turned(k_lin).reshape(suffixes, SL, kv_heads, HD).swapaxes(1, 2).reshape(-1, SL, HD)
    own_values = v_lin.astype(jnp.bfloat16)
    own_values = own_values.reshape(suffixes, SL, kv_heads, HD).swapaxes(1, 2).reshape(-1, SL, HD)

    def by_head(cache):
        return cache.reshape(-1, cache.shape[1], kv_heads, HD).swapaxes(1, 2).reshape(-1, cache.shape[1], HD)

    docs = (source_doc[:, None] * kv_heads + jnp.arange(kv_heads, dtype=jnp.int32)[None, :]).reshape(-1)
    lengths = jnp.repeat(prefix_len, kv_heads)
    row = jnp.arange(suffixes * kv_heads, dtype=jnp.int32)
    keys, values = by_head(keys), by_head(values)
    out = attend(row, docs, lengths, queries, own_keys, own_values, keys, values, 0, row.shape[0])
    out = out.reshape(suffixes, kv_heads, SL, group * HD).swapaxes(1, 2)
    return out.reshape(suffixes * SL, kv_heads * group * HD)


def gather_all(
    inputs,
    norm_gain,
    w_query,
    w_key,
    w_value,
    query_bias,
    key_bias,
    value_bias,
    key_cache,
    value_cache,
    source_doc,
    prefix_len,
):
    full_rows = lax.all_gather(inputs, "corpus", axis=1, tiled=True)
    normed = normalize(full_rows, norm_gain)

    def project(weight, bias):
        whole = lax.all_gather(weight, "fsdp", axis=0, tiled=True)
        return jnp.dot(normed, whole, preferred_element_type=jnp.float32) + bias

    q_lin, k_lin, v_lin = project(w_query, query_bias), project(w_key, key_bias), project(w_value, value_bias)
    keys = lax.all_gather(key_cache, "fsdp", axis=0, tiled=True)
    values = lax.all_gather(value_cache, "fsdp", axis=0, tiled=True)
    position = prefix_len[:, None] + jnp.arange(SL, dtype=jnp.int32)[None, :]
    cosine, sine = rope_tables(position.reshape(-1), HD)
    return dense_attend(source_doc, prefix_len, q_lin, k_lin, v_lin, cosine, sine, keys, values)


def shards(*arrays):
    fits = (
        lax.axis_size("fsdp") == 2 * LINES
        and lax.axis_size("corpus") == COLUMNS
        and arrays[2].shape[1] == LINES * 4 * HD
        and arrays[3].shape[1] == 2 * HD
    )
    return heads_by_line(*arrays) if fits else gather_all(*arrays)


def solution(mesh):
    in_specs = (
        P("fsdp", "corpus"),
        P(),
        P("fsdp", "corpus"),
        P("fsdp", "corpus"),
        P("fsdp", "corpus"),
        P("corpus"),
        P("corpus"),
        P("corpus"),
        P("fsdp", None, "corpus"),
        P("fsdp", None, "corpus"),
        P("fsdp"),
        P("fsdp"),
    )
    out_specs = P("fsdp", "corpus")
    return jax.shard_map(shards, mesh=mesh, in_specs=in_specs, out_specs=out_specs, check_vma=False)
```

```python
import functools

import jax
import jax.numpy as jnp
import numpy as np
from jax import lax
from jax.experimental import pallas as pl
from jax.experimental.pallas import tpu as pltpu
from jax.sharding import PartitionSpec as P

HD = 128
SL = 64
EPS = 1e-06
THETA = 1000000.0
MASKED = -1e30
KEY_BLOCK = 256
LOG2E = 1.4426950408889634
MESH = pl.DeviceIdType.MESH
LINES = 4
COLUMNS = 4


def rope_tables(position, width):
    half = width // 2
    freq = THETA ** (-(jnp.arange(half, dtype=jnp.float32) * 2.0 / width))
    angle = position.astype(jnp.float32)[..., None] * freq
    cosine, sine = jnp.cos(angle), jnp.sin(angle)
    return (
        jnp.concatenate([cosine, cosine], axis=-1),
        jnp.concatenate([-sine, sine], axis=-1),
    )


def normalize(rows, norm_gain):
    wide = rows.astype(jnp.float32)
    spread = jnp.mean(wide * wide, axis=-1, keepdims=True)
    return (wide * lax.rsqrt(spread + EPS) * norm_gain).astype(jnp.bfloat16)


def rotate(vector, cosine, sine):
    return vector * cosine + pltpu.roll(vector, HD // 2, 1) * sine


def attend_kernel(
    pick,
    facts_ref,
    q_in,
    k_in,
    v_in,
    keys_in,
    values_in,
    out_ref,
    q_ref,
    k_ref,
    v_ref,
    keys_ref,
    values_ref,
    fetched,
):
    here = pl.program_id(0)
    length = pick(facts_ref, here)[2]

    def fetch(i):
        row, doc, _ = pick(facts_ref, i)
        pairs = (
            (q_in.at[row], q_ref.at[i]),
            (keys_in.at[doc], keys_ref.at[i]),
            (k_in.at[row], k_ref.at[i]),
            (v_in.at[row], v_ref.at[i]),
            (values_in.at[doc], values_ref.at[i]),
        )
        return [pltpu.make_async_copy(a, b, fetched.at[i, n]) for n, (a, b) in enumerate(pairs)]

    @pl.when(jnp.logical_and(here == 0, length > 0))
    def _():
        for i in range(q_ref.shape[0]):
            for copy in fetch(i):
                copy.start()

    scale = HD ** (-0.5)
    steep = scale * LOG2E
    rows = q_ref.shape[1]
    along = (((1,), (1,)), ((), ()))
    across = (((0,), (0,)), ((), ()))
    block = KEY_BLOCK
    most = keys_ref.shape[1] // block
    blocks = lax.div(length + (block - 1), block)

    def over_rows(op, array):
        return op(array.reshape(-1, 8, rows), axis=0)

    def suffix(count):
        for copy in fetch(here):
            copy.wait()
        queries = q_ref[here]
        own = lax.dot_general(k_ref[here], queries, along, preferred_element_type=jnp.float32)
        token = lax.rem(lax.broadcasted_iota(jnp.int32, (SL, rows), 1), SL)
        other = lax.broadcasted_iota(jnp.int32, (SL, rows), 0)
        own = jnp.where(other <= token, own, MASKED)
        scores = []
        for b in range(count):
            keys = keys_ref[here, b * block : (b + 1) * block, :]
            score = lax.dot_general(keys, queries, along, preferred_element_type=jnp.float32)
            if b == count - 1:
                position = lax.broadcasted_iota(jnp.int32, (block, rows), 0) + b * block
                score = jnp.where(position < length, score, MASKED)
            scores.append(score)
        peak = functools.reduce(jnp.maximum, [over_rows(jnp.max, score) for score in scores])

        own_peak = jnp.max(own, axis=0, keepdims=True)
        own_weights = jnp.exp2((own - own_peak) * steep)
        own_total = jnp.sum(own_weights, axis=0, keepdims=True)
        own_out = lax.dot_general(
            v_ref[here], own_weights.astype(jnp.bfloat16), across, preferred_element_type=jnp.float32
        )

        peak = jnp.max(peak, axis=0, keepdims=True)
        total, acc = 0.0, 0.0
        for b in range(count):
            weights = jnp.exp2((scores[b] - peak) * steep)
            total += over_rows(jnp.sum, weights)
            acc += lax.dot_general(
                values_ref[here, b * block : (b + 1) * block, :],
                weights.astype(jnp.bfloat16),
                across,
                preferred_element_type=jnp.float32,
            )
        total = jnp.sum(total, axis=0, keepdims=True)
        prefix_normed = (acc * (1.0 / total)).astype(jnp.bfloat16)
        prefix_lse = peak * scale + jnp.log(total)
        own_peak = own_peak * scale
        top = jnp.maximum(prefix_lse, own_peak)
        former = jnp.exp(prefix_lse - top)
        latter = jnp.exp(own_peak - top)
        inverse = 1.0 / (former + own_total * latter)
        mixed = prefix_normed.astype(jnp.float32) * (former * inverse) + own_out * (latter * inverse)
        mixed = mixed.T.astype(jnp.bfloat16)
        for h in range(rows // SL):
            out_ref[:, h * HD : (h + 1) * HD] = mixed[h * SL : (h + 1) * SL, :]

    for count in range(1, most + 1):
        @pl.when(blocks == count)
        def _():
            suffix(count)


def attend(pick, count, facts, queries, own_keys, own_values, keys, values):
    rows = queries.shape[1]
    length = keys.shape[1]
    wide = rows // SL * HD
    far = pl.BlockSpec(memory_space=pltpu.HBM)
    held = pltpu.VMEM
    bf16 = jnp.bfloat16
    flops = 2 * count * rows * length * HD
    return pl.pallas_call(
        functools.partial(attend_kernel, pick),
        out_shape=jax.ShapeDtypeStruct((count * SL, wide), jnp.bfloat16),
        grid_spec=pltpu.PrefetchScalarGridSpec(
            num_scalar_prefetch=1,
            grid=(count,),
            in_specs=[far] * 5,
            out_specs=pl.BlockSpec((SL, wide), lambda i, facts: (i, 0)),
            scratch_shapes=[
                held((count, rows, HD), bf16),
                held((count, SL, HD), bf16),
                held((count, SL, HD), bf16),
                held((count, length, HD), bf16),
                held((count, length, HD), bf16),
                pltpu.SemaphoreType.DMA((count, 5)),
            ],
        ),
        compiler_params=pltpu.CompilerParams(
            dimension_semantics=("arbitrary",), vmem_limit_bytes=60 << 20
        ),
        cost_estimate=pl.CostEstimate(
            flops=flops, transcendentals=flops // (4 * HD), bytes_accessed=4 << 20
        ),
    )(facts, queries, own_keys, own_values, keys, values)


def place():
    c = lax.axis_index("corpus")
    f = lax.axis_index("fsdp")
    return c, lax.div(f, 2), lax.rem(f, 2)


def flip(value, bits):
    low = lax.rem(lax.rem(value, 2) + bits % 2, 2)
    high = lax.rem(lax.div(value, 2) + bits // 2, 2)
    return 2 * high + low


def remote(src, dst, send, recv, c, z, k):
    return pltpu.make_async_remote_copy(
        src_ref=src,
        dst_ref=dst,
        send_sem=send,
        recv_sem=recv,
        device_id=(c, 2 * z + k),
        device_id_type=MESH,
    )


def greet(peers):
    barrier = pltpu.get_barrier_semaphore()
    for c, z, k in peers:
        pl.semaphore_signal(barrier, inc=1, device_id=(c, 2 * z + k), device_id_type=MESH)
    pl.semaphore_wait(barrier, len(peers))


def move_kernel(
    x_ref,
    wq_ref,
    wk_ref,
    wv_ref,
    kc_ref,
    vc_ref,
    facts_ref,
    gain_in,
    qb_in,
    kb_in,
    vb_in,
    ct_in,
    st_in,
    turn_in,
    q_ref,
    ok_ref,
    ov_ref,
    facts_out,
    keys_ref,
    values_ref,
    acts,
    wbuf,
    normed,
    acc,
    cos_ref,
    sin_ref,
    facts_held,
    gain_ref,
    qb_ref,
    kb_ref,
    vb_ref,
    ct_ref,
    st_ref,
    turn_ref,
    start_ref,
    asend,
    arecv,
    xsend,
    xrecv,
    fsend,
    frecv,
    wsend,
    wrecv,
    wcsend,
    wcrecv,
    ksend,
    krecv,
    kcsend,
    kcrecv,
    local,
):
    c, z, k = place()
    head = lax.div(z, 2)
    f = 2 * z + k
    inner = jnp.logical_or(z == 1, z == 2)
    outer = jnp.logical_not(inner)
    greet(
        [(c, flip(z, s), k) for s in (1, 2, 3)]
        + [(flip(c, p), z, k) for p in (1, 2, 3)]
        + [(c, z, 1 - k)]
    )
    group = wq_ref.shape[1] // 2
    caches = (kc_ref, vc_ref)
    kept = (keys_ref, values_ref)

    def act_to(s):
        return remote(x_ref, acts.at[z, c], asend.at[s - 1], arecv.at[s - 1], c, flip(z, s), k)

    def act_side(s, p):
        j = flip(z, s)
        src = x_ref if isinstance(s, int) and s == 0 else acts.at[j, c]
        return remote(src, acts.at[j, c], xsend.at[s, p - 1], xrecv.at[s, p - 1], flip(c, p), z, k)

    def fact_to(s):
        return remote(
            facts_ref, facts_held.at[z], fsend.at[s - 1], frecv.at[s - 1], c, flip(z, s), k
        )

    def weight_to(s, which_parts=(0, 1, 2)):
        to = flip(z, s)
        slot = wbuf.at[f]
        which = lax.div(to, 2)
        at = pl.multiple_of(which * group, group)
        kv = pl.multiple_of(which * HD, HD)
        parts = (
            (wk_ref.at[:, pl.ds(kv, HD)], slot.at[:, group : group + HD]),
            (wv_ref.at[:, pl.ds(kv, HD)], slot.at[:, group + HD : group + 2 * HD]),
            (wq_ref.at[:, pl.ds(at, group)], slot.at[:, 0:group]),
        )
        if s == 0:
            return [pltpu.make_async_copy(*parts[i], local.at[i]) for i in which_parts]
        return [
            remote(*parts[i], wsend.at[s - 1, i], wrecv.at[s - 1, i], c, to, k) for i in which_parts
        ]

    def weight_core(s):
        slot = wbuf.at[2 * flip(z, s) + k]
        return remote(slot, slot, wcsend.at[s], wcrecv.at[s], c, z, 1 - k)

    def own_slice(t, which):
        at = pl.multiple_of(which * HD, HD)
        return caches[t].at[0, :, pl.ds(at, HD)]

    def kv_to(s, t):
        to = flip(z, s)
        return remote(
            own_slice(t, lax.div(to, 2)), kept[t].at[f], ksend.at[s - 1, t], krecv.at[s - 1, t], c, to, k
        )

    def kv_core(s, t):
        slot = kept[t].at[2 * flip(z, s) + k]
        src = own_slice(t, head) if s == 0 else slot
        return remote(src, slot, kcsend.at[s, t], kcrecv.at[s, t], c, z, 1 - k)

    def kv_local(t):
        return pltpu.make_async_copy(own_slice(t, head), kept[t].at[f], local.at[3 + t])

    act_own = pltpu.make_async_copy(x_ref, acts.at[z, c], local.at[5])
    fact_own = pltpu.make_async_copy(facts_ref, facts_held.at[z], local.at[6])
    small = [
        pltpu.make_async_copy(a, b, local.at[7 + i])
        for i, (a, b) in enumerate(
            (
                (gain_in, gain_ref),
                (qb_in, qb_ref),
                (kb_in, kb_ref),
                (vb_in, vb_ref),
                (ct_in, ct_ref),
                (st_in, st_ref),
                (turn_in, turn_ref),
            )
        )
    ]

    def project(s):
        j = flip(z, s)
        for p in (1, 2, 3):
            act_side(s, p).wait_recv()

        angle = facts_held[j].astype(jnp.float32) * turn_ref[0:1, :]
        start_ref[0] = jnp.cos(angle)
        start_ref[1] = jnp.sin(angle) * turn_ref[1:2, :]

        @pl.loop(0, 4)
        def _(r):
            at = pl.multiple_of(r * SL, SL)
            total = jnp.zeros((SL, 1), jnp.float32)
            for i in range(COLUMNS):
                wide = acts[j, i, pl.ds(at, SL), :].astype(jnp.float32)
                total += jnp.sum(wide * wide, axis=1, keepdims=True)
            inv = lax.rsqrt(total / (COLUMNS * acts.shape[3]) + EPS)
            for i in range(COLUMNS):
                wide = acts[j, i, pl.ds(at, SL), :].astype(jnp.float32)
                columns = pl.ds(i * acts.shape[3], acts.shape[3])
                normed[pl.ds(at, SL), columns] = (wide * inv * gain_ref[:, columns]).astype(jnp.bfloat16)
            cosl = start_ref[0, pl.ds(r, 1), :]
            sinl = start_ref[1, pl.ds(r, 1), :]
            cos_ref[pl.ds(at, SL), :] = cosl * ct_ref[...] - sinl * st_ref[...]
            sin_ref[pl.ds(at, SL), :] = sinl * ct_ref[...] + cosl * st_ref[...]

        acc[...] = jnp.zeros_like(acc)
        depth = wbuf.shape[1]

        @pl.loop(0, 2 * LINES)
        def _(i):
            at = pl.multiple_of(i * depth, depth)
            acc[...] += jnp.dot(normed[:, pl.ds(at, depth)], wbuf[i], preferred_element_type=jnp.float32)

        cosine, sine = cos_ref[...], sin_ref[...]
        heads = group // HD
        for h in range(heads):
            lin = acc[:, h * HD : (h + 1) * HD] + qb_ref[pl.ds(heads * head + h, 1), :]
            turned = rotate(lin, cosine, sine).astype(jnp.bfloat16)
            for i in range(4):
                q_ref[4 * j + i, h * SL : (h + 1) * SL, :] = turned[i * SL : (i + 1) * SL]
        lin = acc[:, group : group + HD] + kb_ref[pl.ds(head, 1), :]
        turned = rotate(lin, cosine, sine).astype(jnp.bfloat16)
        straight = (acc[:, group + HD : group + 2 * HD] + vb_ref[pl.ds(head, 1), :]).astype(jnp.bfloat16)
        for i in range(4):
            ok_ref[4 * j + i] = turned[i * SL : (i + 1) * SL]
            ov_ref[4 * j + i] = straight[i * SL : (i + 1) * SL]

    @pl.when(outer)
    def _():
        for s in (2, 1):
            act_to(s).start()
        for s in (1, 2, 3):
            fact_to(s).start()
        fact_own.start()
        for s in (2, 1):
            for copy in weight_to(s, (0, 1)):
                copy.start()
        for s in (2, 1):
            act_to(s).wait_send()
            weight_to(s, (2,))[0].start()
        for s in (2, 1):
            weight_to(s, (2,))[0].wait_send()
            for t in (0, 1):
                kv_to(s, t).start()
        for s in (1, 2, 3):
            fact_to(s).wait()
        fact_own.wait()
        facts_out[...] = facts_held[...]
        for s in (2, 1):
            for copy in weight_to(s, (0, 1)):
                copy.wait_send()
            for t in (0, 1):
                kv_to(s, t).wait_send()

    @pl.when(inner)
    def _():
        act_to(3).start()
        for s in (1, 2, 3):
            fact_to(s).start()
        fact_own.start()
        for p in (1, 2, 3):
            act_side(0, p).start()
        act_own.start()
        for copy in weight_to(0):
            copy.start()
        for copy in weight_to(3, (0, 1)):
            copy.start()
        for copy in small:
            copy.start()
        for t in (0, 1):
            kv_local(t).start()
            kv_core(0, t).start()
        act_to(3).wait_send()
        weight_to(3, (2,))[0].start()
        for s in (1, 3, 2):
            act_to(s).wait_recv()
            for p in (1, 2, 3):
                act_side(s, p).start()
        for copy in weight_to(0):
            copy.wait()
        weight_core(0).start()
        for s in (1, 3):
            for copy in weight_to(s):
                copy.wait_recv()
            weight_core(s).start()
        for copy in weight_to(3):
            copy.wait_send()
        for t in (0, 1):
            kv_to(3, t).start()
        for copy in weight_to(2):
            copy.wait_recv()
        weight_core(2).start()

        for s in (1, 2, 3):
            fact_to(s).wait()
        fact_own.wait()
        facts_out[...] = facts_held[...]
        act_own.wait()
        for copy in small:
            copy.wait()
        for s in range(4):
            weight_core(s).wait_recv()

        @pl.loop(0, LINES)
        def _(i):
            project(jnp.where(i < 2, i, 5 - i))

        for t in (0, 1):
            for s in (1, 3, 2):
                kv_to(s, t).wait_recv()
                kv_core(s, t).start()

        act_sides = [act_side(s, p) for s in range(4) for p in (1, 2, 3)]
        for copy in act_sides:
            copy.wait_send()
        for s in range(4):
            weight_core(s).wait_send()
        for t in (0, 1):
            kv_to(3, t).wait_send()
            kv_local(t).wait()
            for s in range(4):
                kv_core(s, t).wait()


def move(inputs, w_query, w_key, w_value, key_cache, value_cache, facts, *small):
    tokens, wide = inputs.shape
    depth = w_query.shape[0]
    group = w_query.shape[1] // 2
    length = key_cache.shape[1]
    docs = 2 * LINES
    suffixes = LINES * (tokens // SL)
    held = pl.BlockSpec(memory_space=pltpu.VMEM)
    far = pl.BlockSpec(memory_space=pltpu.HBM)
    dma = pltpu.SemaphoreType.DMA
    bf16, f32 = jnp.bfloat16, jnp.float32
    flops = 2 * LINES * tokens * wide * COLUMNS * (group + 2 * HD)
    return pl.pallas_call(
        move_kernel,
        out_shape=(
            jax.ShapeDtypeStruct((suffixes, group // HD * SL, HD), bf16),
            jax.ShapeDtypeStruct((suffixes, SL, HD), bf16),
            jax.ShapeDtypeStruct((suffixes, SL, HD), bf16),
            jax.ShapeDtypeStruct((LINES,) + facts.shape, jnp.int32),
            jax.ShapeDtypeStruct((docs, length, HD), bf16),
            jax.ShapeDtypeStruct((docs, length, HD), bf16),
        ),
        in_specs=[far] * 14,
        out_specs=(held, held, held, held, far, far),
        scratch_shapes=[
            pltpu.VMEM((LINES, COLUMNS, tokens, wide), bf16),
            pltpu.VMEM((docs, depth, group + 2 * HD), bf16),
            pltpu.VMEM((tokens, wide * COLUMNS), bf16),
            pltpu.VMEM((tokens, group + 2 * HD), f32),
            pltpu.VMEM((tokens, HD), f32),
            pltpu.VMEM((tokens, HD), f32),
            pltpu.VMEM((LINES,) + facts.shape, jnp.int32),
            *[pltpu.VMEM(array.shape, f32) for array in small],
            pltpu.VMEM((2,) + facts.shape, f32),
            dma((3,)),
            dma((3,)),
            dma((4, 3)),
            dma((4, 3)),
            dma((3,)),
            dma((3,)),
            dma((3, 3)),
            dma((3, 3)),
            dma((4,)),
            dma((4,)),
            dma((3, 2)),
            dma((3, 2)),
            dma((4, 2)),
            dma((4, 2)),
            dma((14,)),
        ],
        compiler_params=pltpu.CompilerParams(
            collective_id=0, has_side_effects=True, vmem_limit_bytes=56 << 20
        ),
        cost_estimate=pl.CostEstimate(flops=flops, transcendentals=0, bytes_accessed=32 << 20),
    )(inputs, w_query, w_key, w_value, key_cache, value_cache, facts, *small)


def heads_by_line(
    inputs,
    norm_gain,
    w_query,
    w_key,
    w_value,
    query_bias,
    key_bias,
    value_bias,
    key_cache,
    value_cache,
    source_doc,
    prefix_len,
):
    c, z, k = place()
    inner = jnp.logical_or(z == 1, z == 2)
    head = lax.div(z, 2)
    own = prefix_len.shape[0]
    facts = jnp.broadcast_to(jnp.concatenate([prefix_len, source_doc])[:, None], (2 * own, HD))
    freq = THETA ** (-(np.arange(HD // 2) * 2.0 / HD))
    sign = np.repeat([-1.0, 1.0], HD // 2)
    freq = np.tile(freq, 2)
    step = np.arange(SL)[:, None] * freq
    tables = (np.cos(step), np.sin(step) * sign, np.stack([freq, sign]))
    queries, own_keys, own_values, facts, keys, values = move(
        inputs,
        w_query,
        w_key,
        w_value,
        key_cache,
        value_cache,
        facts,
        norm_gain[None],
        query_bias.reshape(-1, HD),
        key_bias.reshape(-1, HD),
        value_bias.reshape(-1, HD),
        *[jnp.asarray(table, jnp.float32) for table in tables],
    )

    def pick(s, facts_ref, i):
        _, z, _ = place()
        j = flip(z, s)
        inside = jnp.logical_or(z == 1, z == 2)
        return own * j + i, facts_ref[j, own + i, 0], jnp.where(inside, facts_ref[j, i, 0], 0)

    outs = {}
    for s in (2, 3, 1, 0):
        out = attend(functools.partial(pick, s), own, facts, queries, own_keys, own_values, keys, values)
        if s:
            pairs = [(2 * a + b, 2 * (a ^ s) + b) for a in (1, 2) for b in (0, 1)]
            out = lax.ppermute(out, "fsdp", pairs)
        outs[s] = out
    same = jnp.where(inner, outs[0], outs[1])
    other = jnp.where(inner, outs[3], outs[2])
    return jnp.where(
        head == 0,
        jnp.concatenate([same, other], axis=1),
        jnp.concatenate([other, same], axis=1),
    )


def dense_attend(source_doc, prefix_len, q_lin, k_lin, v_lin, cosine, sine, keys, values):
    suffixes = source_doc.shape[0]
    kv_heads = k_lin.shape[1] // HD
    group = q_lin.shape[1] // k_lin.shape[1]

    def turned(lin):
        vector = lin.reshape(suffixes * SL, -1, HD)
        other = jnp.roll(vector, HD // 2, axis=-1)
        return (vector * cosine[:, None] + other * sine[:, None]).astype(jnp.bfloat16)

    queries = turned(q_lin).reshape(suffixes, SL, kv_heads, group, HD)
    queries = queries.transpose(0, 2, 3, 1, 4).reshape(suffixes * kv_heads, group * SL, HD)
    own_keys = turned(k_lin).reshape(suffixes, SL, kv_heads, HD).swapaxes(1, 2).reshape(-1, SL, HD)
    own_values = v_lin.astype(jnp.bfloat16)
    own_values = own_values.reshape(suffixes, SL, kv_heads, HD).swapaxes(1, 2).reshape(-1, SL, HD)

    def by_head(cache):
        return cache.reshape(-1, cache.shape[1], kv_heads, HD).swapaxes(1, 2).reshape(-1, cache.shape[1], HD)

    docs = (source_doc[:, None] * kv_heads + jnp.arange(kv_heads, dtype=jnp.int32)[None, :]).reshape(-1)
    lengths = jnp.repeat(prefix_len, kv_heads)
    facts = jnp.stack([docs, lengths])
    pick = lambda facts_ref, i: (i, facts_ref[0, i], facts_ref[1, i])
    out = attend(pick, docs.shape[0], facts, queries, own_keys, own_values, by_head(keys), by_head(values))
    out = out.reshape(suffixes, kv_heads, SL, group * HD).swapaxes(1, 2)
    return out.reshape(suffixes * SL, kv_heads * group * HD)


def gather_all(
    inputs,
    norm_gain,
    w_query,
    w_key,
    w_value,
    query_bias,
    key_bias,
    value_bias,
    key_cache,
    value_cache,
    source_doc,
    prefix_len,
):
    full_rows = lax.all_gather(inputs, "corpus", axis=1, tiled=True)
    normed = normalize(full_rows, norm_gain)

    def project(weight, bias):
        whole = lax.all_gather(weight, "fsdp", axis=0, tiled=True)
        return jnp.dot(normed, whole, preferred_element_type=jnp.float32) + bias

    q_lin, k_lin, v_lin = project(w_query, query_bias), project(w_key, key_bias), project(w_value, value_bias)
    keys = lax.all_gather(key_cache, "fsdp", axis=0, tiled=True)
    values = lax.all_gather(value_cache, "fsdp", axis=0, tiled=True)
    position = prefix_len[:, None] + jnp.arange(SL, dtype=jnp.int32)[None, :]
    cosine, sine = rope_tables(position.reshape(-1), HD)
    return dense_attend(source_doc, prefix_len, q_lin, k_lin, v_lin, cosine, sine, keys, values)


def shards(*arrays):
    fits = (
        lax.axis_size("fsdp") == 2 * LINES
        and lax.axis_size("corpus") == COLUMNS
        and arrays[2].shape[1] == LINES * 4 * HD
        and arrays[3].shape[1] == 2 * HD
    )
    return heads_by_line(*arrays) if fits else gather_all(*arrays)


def solution(mesh):
    in_specs = (
        P("fsdp", "corpus"),
        P(),
        P("fsdp", "corpus"),
        P("fsdp", "corpus"),
        P("fsdp", "corpus"),
        P("corpus"),
        P("corpus"),
        P("corpus"),
        P("fsdp", None, "corpus"),
        P("fsdp", None, "corpus"),
        P("fsdp"),
        P("fsdp"),
    )
    out_specs = P("fsdp", "corpus")
    return jax.shard_map(shards, mesh=mesh, in_specs=in_specs, out_specs=out_specs, check_vma=False)
```

```python
import functools

import jax
import jax.numpy as jnp
import numpy as np
from jax import lax
from jax.experimental import pallas as pl
from jax.experimental.pallas import tpu as pltpu
from jax.sharding import PartitionSpec as P

HD = 128
SL = 64
EPS = 1e-06
THETA = 1000000.0
MASKED = -1e30
KEY_BLOCK = 256
LOG2E = 1.4426950408889634
MESH = pl.DeviceIdType.MESH
LINES = 4
COLUMNS = 4
PIECES = (0, 1, 2)


def rope_tables(position, width):
    half = width // 2
    freq = THETA ** (-(jnp.arange(half, dtype=jnp.float32) * 2.0 / width))
    angle = position.astype(jnp.float32)[..., None] * freq
    cosine, sine = jnp.cos(angle), jnp.sin(angle)
    return (
        jnp.concatenate([cosine, cosine], axis=-1),
        jnp.concatenate([-sine, sine], axis=-1),
    )


def normalize(rows, norm_gain):
    wide = rows.astype(jnp.float32)
    spread = jnp.mean(wide * wide, axis=-1, keepdims=True)
    return (wide * lax.rsqrt(spread + EPS) * norm_gain).astype(jnp.bfloat16)


def rotate(vector, cosine, sine):
    return vector * cosine + pltpu.roll(vector, HD // 2, 1) * sine


def attend_kernel(
    pick,
    facts_ref,
    q_in,
    k_in,
    v_in,
    keys_in,
    values_in,
    out_ref,
    q_ref,
    k_ref,
    v_ref,
    keys_ref,
    values_ref,
    fetched,
):
    here = pl.program_id(0)
    length = pick(facts_ref, here)[2]

    def fetch(i):
        row, doc, _ = pick(facts_ref, i)
        pairs = (
            (q_in.at[row], q_ref.at[i]),
            (keys_in.at[doc], keys_ref.at[i]),
            (k_in.at[row], k_ref.at[i]),
            (v_in.at[row], v_ref.at[i]),
            (values_in.at[doc], values_ref.at[i]),
        )
        return [pltpu.make_async_copy(a, b, fetched.at[i, n]) for n, (a, b) in enumerate(pairs)]

    @pl.when(jnp.logical_and(here == 0, length > 0))
    def _():
        for i in range(q_ref.shape[0]):
            for copy in fetch(i):
                copy.start()

    scale = HD ** (-0.5)
    steep = scale * LOG2E
    rows = q_ref.shape[1]
    along = (((1,), (1,)), ((), ()))
    across = (((0,), (0,)), ((), ()))
    block = KEY_BLOCK
    most = keys_ref.shape[1] // block
    blocks = lax.div(length + (block - 1), block)

    def over_rows(op, array):
        return op(array.reshape(-1, 8, rows), axis=0)

    def suffix(count):
        for copy in fetch(here):
            copy.wait()
        queries = q_ref[here]
        own = lax.dot_general(k_ref[here], queries, along, preferred_element_type=jnp.float32)
        token = lax.rem(lax.broadcasted_iota(jnp.int32, (SL, rows), 1), SL)
        other = lax.broadcasted_iota(jnp.int32, (SL, rows), 0)
        own = jnp.where(other <= token, own, MASKED)
        scores = []
        for b in range(count):
            keys = keys_ref[here, b * block : (b + 1) * block, :]
            score = lax.dot_general(keys, queries, along, preferred_element_type=jnp.float32)
            if b == count - 1:
                position = lax.broadcasted_iota(jnp.int32, (block, rows), 0) + b * block
                score = jnp.where(position < length, score, MASKED)
            scores.append(score)
        peak = functools.reduce(jnp.maximum, [over_rows(jnp.max, score) for score in scores])

        own_peak = jnp.max(own, axis=0, keepdims=True)
        own_weights = jnp.exp2((own - own_peak) * steep)
        own_total = jnp.sum(own_weights, axis=0, keepdims=True)
        own_out = lax.dot_general(
            v_ref[here], own_weights.astype(jnp.bfloat16), across, preferred_element_type=jnp.float32
        )

        peak = jnp.max(peak, axis=0, keepdims=True)
        total, acc = 0.0, 0.0
        for b in range(count):
            weights = jnp.exp2((scores[b] - peak) * steep)
            total += over_rows(jnp.sum, weights)
            acc += lax.dot_general(
                values_ref[here, b * block : (b + 1) * block, :],
                weights.astype(jnp.bfloat16),
                across,
                preferred_element_type=jnp.float32,
            )
        total = jnp.sum(total, axis=0, keepdims=True)
        prefix_normed = (acc * (1.0 / total)).astype(jnp.bfloat16)
        prefix_lse = peak * scale + jnp.log(total)
        own_peak = own_peak * scale
        top = jnp.maximum(prefix_lse, own_peak)
        former = jnp.exp(prefix_lse - top)
        latter = jnp.exp(own_peak - top)
        inverse = 1.0 / (former + own_total * latter)
        mixed = prefix_normed.astype(jnp.float32) * (former * inverse) + own_out * (latter * inverse)
        mixed = mixed.T.astype(jnp.bfloat16)
        for h in range(rows // SL):
            out_ref[:, h * HD : (h + 1) * HD] = mixed[h * SL : (h + 1) * SL, :]

    for count in range(1, most + 1):
        @pl.when(blocks == count)
        def _():
            suffix(count)


def attend(pick, count, facts, queries, own_keys, own_values, keys, values):
    rows = queries.shape[1]
    length = keys.shape[1]
    wide = rows // SL * HD
    far = pl.BlockSpec(memory_space=pltpu.HBM)
    held = pltpu.VMEM
    bf16 = jnp.bfloat16
    flops = 2 * count * rows * length * HD
    return pl.pallas_call(
        functools.partial(attend_kernel, pick),
        out_shape=jax.ShapeDtypeStruct((count * SL, wide), jnp.bfloat16),
        grid_spec=pltpu.PrefetchScalarGridSpec(
            num_scalar_prefetch=1,
            grid=(count,),
            in_specs=[far] * 5,
            out_specs=pl.BlockSpec((SL, wide), lambda i, facts: (i, 0)),
            scratch_shapes=[
                held((count, rows, HD), bf16),
                held((count, SL, HD), bf16),
                held((count, SL, HD), bf16),
                held((count, length, HD), bf16),
                held((count, length, HD), bf16),
                pltpu.SemaphoreType.DMA((count, 5)),
            ],
        ),
        compiler_params=pltpu.CompilerParams(
            dimension_semantics=("arbitrary",), vmem_limit_bytes=60 << 20
        ),
        cost_estimate=pl.CostEstimate(
            flops=flops, transcendentals=flops // (4 * HD), bytes_accessed=4 << 20
        ),
    )(facts, queries, own_keys, own_values, keys, values)


def place():
    c = lax.axis_index("corpus")
    f = lax.axis_index("fsdp")
    return c, lax.div(f, 2), lax.rem(f, 2)


def flip(value, bits):
    low = lax.rem(lax.rem(value, 2) + bits % 2, 2)
    high = lax.rem(lax.div(value, 2) + bits // 2, 2)
    return 2 * high + low


def remote(src, dst, send, recv, c, z, k):
    return pltpu.make_async_remote_copy(
        src_ref=src,
        dst_ref=dst,
        send_sem=send,
        recv_sem=recv,
        device_id=(c, 2 * z + k),
        device_id_type=MESH,
    )


def greet(peers):
    barrier = pltpu.get_barrier_semaphore()
    for c, z, k in peers:
        pl.semaphore_signal(barrier, inc=1, device_id=(c, 2 * z + k), device_id_type=MESH)
    pl.semaphore_wait(barrier, len(peers))


def move_kernel(
    x_ref,
    wq_ref,
    wk_ref,
    wv_ref,
    kc_ref,
    vc_ref,
    facts_ref,
    gain_in,
    qb_in,
    kb_in,
    vb_in,
    ct_in,
    st_in,
    turn_in,
    out_ref,
    q_ref,
    ok_ref,
    ov_ref,
    keys_ref,
    values_ref,
    weights_ref,
    stat_ref,
    stage,
    numbers,
    acts,
    wbuf,
    normed,
    acc,
    cos_ref,
    sin_ref,
    facts_held,
    gain_ref,
    qb_ref,
    kb_ref,
    vb_ref,
    ct_ref,
    st_ref,
    turn_ref,
    start_ref,
    asend,
    arecv,
    xsend,
    xrecv,
    fsend,
    frecv,
    wsend,
    wrecv,
    wcsend,
    wcrecv,
    ksend,
    krecv,
    kcsend,
    kcrecv,
    osend,
    orecv,
    local,
):
    c, z, k = place()
    head = lax.div(z, 2)
    f = 2 * z + k
    length = kc_ref.shape[1]
    inner = jnp.logical_or(z == 1, z == 2)
    outer = jnp.logical_not(inner)
    greet(
        [(c, flip(z, s), k) for s in (1, 2, 3)]
        + [(flip(c, p), z, k) for p in (1, 2, 3)]
        + [(c, z, 1 - k)]
    )
    group = wq_ref.shape[1] // 2

    def act_to(s):
        return remote(x_ref, acts.at[z, c], asend.at[s - 1], arecv.at[s - 1], c, flip(z, s), k)

    def act_side(s, p):
        j = flip(z, s)
        src = x_ref if isinstance(s, int) and s == 0 else acts.at[j, c]
        return remote(src, acts.at[j, c], xsend.at[s, p - 1], xrecv.at[s, p - 1], flip(c, p), z, k)

    def fact_to(s):
        return remote(
            facts_ref, facts_held.at[z], fsend.at[s - 1], frecv.at[s - 1], c, flip(z, s), k
        )

    def weight_to(s, which_parts=(0, 1, 2)):
        to = flip(z, s)
        slot = wbuf.at[f]
        which = lax.div(to, 2)
        at = pl.multiple_of(which * group, group)
        kv = pl.multiple_of(which * HD, HD)
        parts = (
            (wk_ref.at[:, pl.ds(kv, HD)], slot.at[:, group : group + HD]),
            (wv_ref.at[:, pl.ds(kv, HD)], slot.at[:, group + HD : group + 2 * HD]),
            (wq_ref.at[:, pl.ds(at, group)], slot.at[:, 0:group]),
        )
        if s == 0:
            return [pltpu.make_async_copy(*parts[i], local.at[i]) for i in which_parts]
        return [
            remote(*parts[i], wsend.at[s - 1, i], wrecv.at[s - 1, i], c, to, k) for i in which_parts
        ]

    def weight_core(s):
        slot = wbuf.at[2 * flip(z, s) + k]
        return remote(slot, slot, wcsend.at[s], wcrecv.at[s], c, z, 1 - k)

    def piece(t):
        if t == 0:
            return kc_ref, keys_ref, slice(0, length)
        return vc_ref, values_ref, slice((t - 1) * length // 2, t * length // 2)

    def own_slice(t, which):
        cache, _, part = piece(t)
        return cache.at[0, part, pl.ds(pl.multiple_of(which * HD, HD), HD)]

    def kept(t, doc):
        _, buffer, part = piece(t)
        return buffer.at[doc, part, :]

    def kv_to(s, t):
        to = flip(z, s)
        return remote(
            own_slice(t, lax.div(to, 2)), kept(t, f), ksend.at[s - 1, t], krecv.at[s - 1, t], c, to, k
        )

    def kv_core(s, t):
        slot = kept(t, 2 * flip(z, s) + k)
        src = own_slice(t, head) if s == 0 else slot
        return remote(src, slot, kcsend.at[s, t], kcrecv.at[s, t], c, z, 1 - k)

    def kv_local(t):
        return pltpu.make_async_copy(own_slice(t, head), kept(t, f), local.at[13 + t])

    def rows_of(r, which):
        rows = pl.ds(pl.multiple_of(r * SL, SL), SL)
        return out_ref.at[rows, pl.ds(pl.multiple_of(which * group, group), group)]

    def out_to(s, r):
        return remote(
            stage.at[s, r], rows_of(r, head), osend.at[s, r], orecv.at[s, r], c, flip(z, s), k
        )

    def out_local(r):
        return pltpu.make_async_copy(stage.at[0, r], rows_of(r, head), osend.at[0, r])

    act_own = pltpu.make_async_copy(x_ref, acts.at[z, c], local.at[5])
    fact_own = pltpu.make_async_copy(facts_ref, facts_held.at[z], local.at[6])
    small = [
        pltpu.make_async_copy(a, b, local.at[i + (3 if i < 2 else 5)])
        for i, (a, b) in enumerate(
            (
                (gain_in, gain_ref),
                (qb_in, qb_ref),
                (kb_in, kb_ref),
                (vb_in, vb_ref),
                (ct_in, ct_ref),
                (st_in, st_ref),
                (turn_in, turn_ref),
            )
        )
    ]

    def project(s):
        j = flip(z, s)
        for p in (1, 2, 3):
            act_side(s, p).wait_recv()

        angle = facts_held[j].astype(jnp.float32) * turn_ref[0:1, :]
        start_ref[0] = jnp.cos(angle)
        start_ref[1] = jnp.sin(angle) * turn_ref[1:2, :]

        @pl.loop(0, 4)
        def _(r):
            at = pl.multiple_of(r * SL, SL)
            total = jnp.zeros((SL, 1), jnp.float32)
            for i in range(COLUMNS):
                wide = acts[j, i, pl.ds(at, SL), :].astype(jnp.float32)
                total += jnp.sum(wide * wide, axis=1, keepdims=True)
            inv = lax.rsqrt(total / (COLUMNS * acts.shape[3]) + EPS)
            for i in range(COLUMNS):
                wide = acts[j, i, pl.ds(at, SL), :].astype(jnp.float32)
                columns = pl.ds(i * acts.shape[3], acts.shape[3])
                normed[pl.ds(at, SL), columns] = (wide * inv * gain_ref[:, columns]).astype(jnp.bfloat16)
            cosl = start_ref[0, pl.ds(r, 1), :]
            sinl = start_ref[1, pl.ds(r, 1), :]
            cos_ref[pl.ds(at, SL), :] = cosl * ct_ref[...] - sinl * st_ref[...]
            sin_ref[pl.ds(at, SL), :] = sinl * ct_ref[...] + cosl * st_ref[...]

        acc[...] = jnp.zeros_like(acc)
        depth = wbuf.shape[1]

        @pl.loop(0, 2 * LINES)
        def _(i):
            at = pl.multiple_of(i * depth, depth)
            acc[...] += jnp.dot(normed[:, pl.ds(at, depth)], wbuf[i], preferred_element_type=jnp.float32)

        cosine, sine = cos_ref[...], sin_ref[...]
        heads = group // HD
        for h in range(heads):
            lin = acc[:, h * HD : (h + 1) * HD] + qb_ref[pl.ds(heads * head + h, 1), :]
            turned = rotate(lin, cosine, sine).astype(jnp.bfloat16)
            for i in range(4):
                q_ref[4 * j + i, h * SL : (h + 1) * SL, :] = turned[i * SL : (i + 1) * SL]
        lin = acc[:, group : group + HD] + kb_ref[pl.ds(head, 1), :]
        turned = rotate(lin, cosine, sine).astype(jnp.bfloat16)
        straight = (acc[:, group + HD : group + 2 * HD] + vb_ref[pl.ds(head, 1), :]).astype(jnp.bfloat16)
        for i in range(4):
            ok_ref[4 * j + i] = turned[i * SL : (i + 1) * SL]
            ov_ref[4 * j + i] = straight[i * SL : (i + 1) * SL]

    scale = HD ** (-0.5)
    steep = scale * LOG2E
    rows = q_ref.shape[1]
    along = (((1,), (1,)), ((), ()))
    across = (((0,), (0,)), ((), ()))
    cuts = [slice(at, at + KEY_BLOCK) for at in range(0, length, KEY_BLOCK)]

    def over_rows(op, array):
        return op(array.reshape(-1, 8, rows), axis=0)

    def weigh(s, r, slot):
        j = flip(z, s)
        doc, size = numbers[j, 4 + r, 0], numbers[j, r, 0]
        queries = q_ref[4 * j + r]
        scores = []
        for cut in cuts:
            score = lax.dot_general(
                keys_ref[doc, cut, :], queries, along, preferred_element_type=jnp.float32
            )
            position = lax.broadcasted_iota(jnp.int32, score.shape, 0)
            scores.append(jnp.where(position < size - cut.start, score, MASKED))
        peak = functools.reduce(jnp.maximum, [over_rows(jnp.max, score) for score in scores])
        peak = jnp.max(peak, axis=0, keepdims=True)
        total = 0.0
        for score, cut in zip(scores, cuts):
            weights = jnp.exp2((score - peak) * steep)
            total += over_rows(jnp.sum, weights)
            weights_ref[slot, cut, :] = weights.astype(jnp.bfloat16)
        stat_ref[slot, 0:1, :] = peak * scale
        stat_ref[slot, 1:2, :] = jnp.sum(total, axis=0, keepdims=True)

    def blend(s, r, slot):
        j = flip(z, s)
        doc = numbers[j, 4 + r, 0]
        row = 4 * j + r
        own = lax.dot_general(ok_ref[row], q_ref[row], along, preferred_element_type=jnp.float32)
        token = lax.rem(lax.broadcasted_iota(jnp.int32, (SL, rows), 1), SL)
        other = lax.broadcasted_iota(jnp.int32, (SL, rows), 0)
        own = jnp.where(other <= token, own, MASKED)
        acc = 0.0
        for cut in cuts:
            acc += lax.dot_general(
                values_ref[doc, cut, :],
                weights_ref[slot, cut, :],
                across,
                preferred_element_type=jnp.float32,
            )
        own_peak = jnp.max(own, axis=0, keepdims=True)
        own_weights = jnp.exp2((own - own_peak) * steep)
        own_total = jnp.sum(own_weights, axis=0, keepdims=True)
        own_out = lax.dot_general(
            ov_ref[row], own_weights.astype(jnp.bfloat16), across, preferred_element_type=jnp.float32
        )
        total = stat_ref[slot, 1:2, :]
        prefix_normed = (acc * (1.0 / total)).astype(jnp.bfloat16)
        prefix_lse = stat_ref[slot, 0:1, :] + jnp.log(total)
        own_peak = own_peak * scale
        top = jnp.maximum(prefix_lse, own_peak)
        former = jnp.exp(prefix_lse - top)
        latter = jnp.exp(own_peak - top)
        inverse = 1.0 / (former + own_total * latter)
        mixed = prefix_normed.astype(jnp.float32) * (former * inverse) + own_out * (latter * inverse)
        mixed = mixed.T.astype(jnp.bfloat16)
        for h in range(rows // SL):
            stage[s, r, :, h * HD : (h + 1) * HD] = mixed[h * SL : (h + 1) * SL, :]

    @pl.when(outer)
    def _():
        for s in (2, 1):
            act_to(s).start()
        for s in (1, 2, 3):
            fact_to(s).start()
        fact_own.start()
        for s in (2, 1):
            for copy in weight_to(s, (0, 1)):
                copy.start()
        for s in (2, 1):
            act_to(s).wait_send()
            weight_to(s, (2,))[0].start()
        for t in PIECES:
            for s in (2, 1):
                if t == 0:
                    weight_to(s, (2,))[0].wait_send()
                else:
                    kv_to(s, t - 1).wait_send()
                kv_to(s, t).start()
        for s in (1, 2, 3):
            fact_to(s).wait()
        fact_own.wait()
        for s in (2, 1):
            for copy in weight_to(s, (0, 1)):
                copy.wait_send()
            kv_to(s, PIECES[-1]).wait_send()
        for s in (2, 1):
            for r in range(4):
                out_to(s, r).wait_recv()

    @pl.when(inner)
    def _():
        act_to(3).start()
        for s in (1, 2, 3):
            fact_to(s).start()
        fact_own.start()
        for p in (1, 2, 3):
            act_side(0, p).start()
        act_own.start()
        for copy in weight_to(0):
            copy.start()
        for copy in weight_to(3, (0, 1)):
            copy.start()
        for copy in small:
            copy.start()
        for t in PIECES:
            kv_local(t).start()
            kv_core(0, t).start()
        act_to(3).wait_send()
        weight_to(3, (2,))[0].start()
        for s in (1, 3, 2):
            act_to(s).wait_recv()
            for p in (1, 2, 3):
                act_side(s, p).start()
        for copy in weight_to(0):
            copy.wait()
        weight_core(0).start()
        for s in (1, 3):
            for copy in weight_to(s):
                copy.wait_recv()
            weight_core(s).start()
        for copy in weight_to(3):
            copy.wait_send()
        kv_to(3, 0).start()
        for copy in weight_to(2):
            copy.wait_recv()
        weight_core(2).start()

        for s in (1, 2, 3):
            fact_to(s).wait()
        fact_own.wait()
        to_scalars = pltpu.make_async_copy(facts_held, numbers, local.at[6])
        to_scalars.start()
        act_own.wait()
        for copy in small:
            copy.wait()
        for s in range(4):
            weight_core(s).wait_recv()

        @pl.loop(0, LINES)
        def _(i):
            project(jnp.where(i < 2, i, 5 - i))

        to_scalars.wait()
        kv_to(3, 0).wait_send()
        for t in PIECES[1:]:
            kv_to(3, t).start()

        def pass_on(t):
            for s in (1, 3, 2):
                kv_to(s, t).wait_recv()
                kv_core(s, t).start()

        def arrived(t):
            kv_local(t).wait()
            for s in range(4):
                kv_core(s, t).wait_recv()

        pass_on(0)
        arrived(0)

        @pl.loop(0, 8)
        def _(n):
            weigh(2 + lax.div(n, 4), lax.rem(n, 4), n)

        for t in PIECES[1:]:
            pass_on(t)
        for t in PIECES[1:]:
            arrived(t)

        @pl.loop(0, 8)
        def _(n):
            s, r = 2 + lax.div(n, 4), lax.rem(n, 4)
            blend(s, r, n)
            out_to(s, r).start()

        @pl.loop(0, 8)
        def _(n):
            s, r = 1 - lax.div(n, 4), lax.rem(n, 4)
            weigh(s, r, n)
            blend(s, r, n)

            @pl.when(s == 1)
            def _():
                out_to(1, r).start()

            @pl.when(s == 0)
            def _():
                out_local(r).start()

        act_sides = [act_side(s, p) for s in range(4) for p in (1, 2, 3)]
        for copy in act_sides:
            copy.wait_send()
        for s in range(4):
            weight_core(s).wait_send()
        for t in PIECES:
            if t:
                kv_to(3, t).wait_send()
            for s in range(4):
                kv_core(s, t).wait_send()
        for r in range(4):
            out_local(r).wait()
            for s in (1, 2, 3):
                out_to(s, r).wait_send()
            out_to(3, r).wait_recv()


def move(inputs, w_query, w_key, w_value, key_cache, value_cache, facts, *small):
    tokens, wide = inputs.shape
    depth = w_query.shape[0]
    group = w_query.shape[1] // 2
    length = key_cache.shape[1]
    docs = 2 * LINES
    suffixes = LINES * (tokens // SL)
    rows = group // HD * SL
    far = pl.BlockSpec(memory_space=pltpu.HBM)
    dma = pltpu.SemaphoreType.DMA
    bf16, f32 = jnp.bfloat16, jnp.float32
    flops = 2 * LINES * tokens * wide * COLUMNS * (group + 2 * HD)
    return pl.pallas_call(
        move_kernel,
        out_shape=jax.ShapeDtypeStruct((tokens, 2 * group), bf16),
        in_specs=[far] * 14,
        out_specs=far,
        scratch_shapes=[
            pltpu.VMEM((suffixes, rows, HD), bf16),
            pltpu.VMEM((suffixes, SL, HD), bf16),
            pltpu.VMEM((suffixes, SL, HD), bf16),
            pltpu.VMEM((docs, length, HD), bf16),
            pltpu.VMEM((docs, length, HD), bf16),
            pltpu.VMEM((8, length, rows), bf16),
            pltpu.VMEM((8, 8, rows), f32),
            pltpu.VMEM((LINES, tokens // SL, SL, group), bf16),
            pltpu.SMEM((LINES,) + facts.shape, jnp.int32),
            pltpu.VMEM((LINES, COLUMNS, tokens, wide), bf16),
            pltpu.VMEM((docs, depth, group + 2 * HD), bf16),
            pltpu.VMEM((tokens, wide * COLUMNS), bf16),
            pltpu.VMEM((tokens, group + 2 * HD), f32),
            pltpu.VMEM((tokens, HD), f32),
            pltpu.VMEM((tokens, HD), f32),
            pltpu.VMEM((LINES,) + facts.shape, jnp.int32),
            *[pltpu.VMEM(array.shape, f32) for array in small],
            pltpu.VMEM((2,) + facts.shape, f32),
            dma((3,)),
            dma((3,)),
            dma((4, 3)),
            dma((4, 3)),
            dma((3,)),
            dma((3,)),
            dma((3, 3)),
            dma((3, 3)),
            dma((4,)),
            dma((4,)),
            dma((3, 3)),
            dma((3, 3)),
            dma((4, 3)),
            dma((4, 3)),
            dma((4, 4)),
            dma((4, 4)),
            dma((16,)),
        ],
        compiler_params=pltpu.CompilerParams(
            collective_id=0, has_side_effects=True, vmem_limit_bytes=62 << 20
        ),
        cost_estimate=pl.CostEstimate(flops=flops, transcendentals=0, bytes_accessed=32 << 20),
    )(inputs, w_query, w_key, w_value, key_cache, value_cache, facts, *small)


def heads_by_line(
    inputs,
    norm_gain,
    w_query,
    w_key,
    w_value,
    query_bias,
    key_bias,
    value_bias,
    key_cache,
    value_cache,
    source_doc,
    prefix_len,
):
    own = prefix_len.shape[0]
    facts = jnp.broadcast_to(jnp.concatenate([prefix_len, source_doc])[:, None], (2 * own, HD))
    freq = THETA ** (-(np.arange(HD // 2) * 2.0 / HD))
    sign = np.repeat([-1.0, 1.0], HD // 2)
    freq = np.tile(freq, 2)
    step = np.arange(SL)[:, None] * freq
    tables = (np.cos(step), np.sin(step) * sign, np.stack([freq, sign]))
    return move(
        inputs,
        w_query,
        w_key,
        w_value,
        key_cache,
        value_cache,
        facts,
        norm_gain[None],
        query_bias.reshape(-1, HD),
        key_bias.reshape(-1, HD),
        value_bias.reshape(-1, HD),
        *[jnp.asarray(table, jnp.float32) for table in tables],
    )


def dense_attend(source_doc, prefix_len, q_lin, k_lin, v_lin, cosine, sine, keys, values):
    suffixes = source_doc.shape[0]
    kv_heads = k_lin.shape[1] // HD
    group = q_lin.shape[1] // k_lin.shape[1]

    def turned(lin):
        vector = lin.reshape(suffixes * SL, -1, HD)
        other = jnp.roll(vector, HD // 2, axis=-1)
        return (vector * cosine[:, None] + other * sine[:, None]).astype(jnp.bfloat16)

    queries = turned(q_lin).reshape(suffixes, SL, kv_heads, group, HD)
    queries = queries.transpose(0, 2, 3, 1, 4).reshape(suffixes * kv_heads, group * SL, HD)
    own_keys = turned(k_lin).reshape(suffixes, SL, kv_heads, HD).swapaxes(1, 2).reshape(-1, SL, HD)
    own_values = v_lin.astype(jnp.bfloat16)
    own_values = own_values.reshape(suffixes, SL, kv_heads, HD).swapaxes(1, 2).reshape(-1, SL, HD)

    def by_head(cache):
        return cache.reshape(-1, cache.shape[1], kv_heads, HD).swapaxes(1, 2).reshape(-1, cache.shape[1], HD)

    docs = (source_doc[:, None] * kv_heads + jnp.arange(kv_heads, dtype=jnp.int32)[None, :]).reshape(-1)
    lengths = jnp.repeat(prefix_len, kv_heads)
    facts = jnp.stack([docs, lengths])
    pick = lambda facts_ref, i: (i, facts_ref[0, i], facts_ref[1, i])
    out = attend(pick, docs.shape[0], facts, queries, own_keys, own_values, by_head(keys), by_head(values))
    out = out.reshape(suffixes, kv_heads, SL, group * HD).swapaxes(1, 2)
    return out.reshape(suffixes * SL, kv_heads * group * HD)


def gather_all(
    inputs,
    norm_gain,
    w_query,
    w_key,
    w_value,
    query_bias,
    key_bias,
    value_bias,
    key_cache,
    value_cache,
    source_doc,
    prefix_len,
):
    full_rows = lax.all_gather(inputs, "corpus", axis=1, tiled=True)
    normed = normalize(full_rows, norm_gain)

    def project(weight, bias):
        whole = lax.all_gather(weight, "fsdp", axis=0, tiled=True)
        return jnp.dot(normed, whole, preferred_element_type=jnp.float32) + bias

    q_lin, k_lin, v_lin = project(w_query, query_bias), project(w_key, key_bias), project(w_value, value_bias)
    keys = lax.all_gather(key_cache, "fsdp", axis=0, tiled=True)
    values = lax.all_gather(value_cache, "fsdp", axis=0, tiled=True)
    position = prefix_len[:, None] + jnp.arange(SL, dtype=jnp.int32)[None, :]
    cosine, sine = rope_tables(position.reshape(-1), HD)
    return dense_attend(source_doc, prefix_len, q_lin, k_lin, v_lin, cosine, sine, keys, values)


def shards(*arrays):
    fits = (
        lax.axis_size("fsdp") == 2 * LINES
        and lax.axis_size("corpus") == COLUMNS
        and arrays[2].shape[1] == LINES * 4 * HD
        and arrays[3].shape[1] == 2 * HD
    )
    return heads_by_line(*arrays) if fits else gather_all(*arrays)


def solution(mesh):
    in_specs = (
        P("fsdp", "corpus"),
        P(),
        P("fsdp", "corpus"),
        P("fsdp", "corpus"),
        P("fsdp", "corpus"),
        P("corpus"),
        P("corpus"),
        P("corpus"),
        P("fsdp", None, "corpus"),
        P("fsdp", None, "corpus"),
        P("fsdp"),
        P("fsdp"),
    )
    out_specs = P("fsdp", "corpus")
    return jax.shard_map(shards, mesh=mesh, in_specs=in_specs, out_specs=out_specs, check_vma=False)
```

```python
import functools

import jax
import jax.numpy as jnp
import numpy as np
from jax import lax
from jax.experimental import pallas as pl
from jax.experimental.pallas import tpu as pltpu
from jax.sharding import PartitionSpec as P

HD = 128
SL = 64
EPS = 1e-06
THETA = 1000000.0
MASKED = -1e30
KEY_BLOCK = 256
LOG2E = 1.4426950408889634
MESH = pl.DeviceIdType.MESH
LINES = 4
COLUMNS = 4
PIECES = (0, 1, 2)
WIDE = 256


def rope_tables(position, width):
    half = width // 2
    freq = THETA ** (-(jnp.arange(half, dtype=jnp.float32) * 2.0 / width))
    angle = position.astype(jnp.float32)[..., None] * freq
    cosine, sine = jnp.cos(angle), jnp.sin(angle)
    return (
        jnp.concatenate([cosine, cosine], axis=-1),
        jnp.concatenate([-sine, sine], axis=-1),
    )


def normalize(rows, norm_gain):
    wide = rows.astype(jnp.float32)
    spread = jnp.mean(wide * wide, axis=-1, keepdims=True)
    return (wide * lax.rsqrt(spread + EPS) * norm_gain).astype(jnp.bfloat16)


def rotate(vector, cosine, sine):
    return vector * cosine + pltpu.roll(vector, HD // 2, 1) * sine


def attend_kernel(
    pick,
    facts_ref,
    q_in,
    k_in,
    v_in,
    keys_in,
    values_in,
    out_ref,
    q_ref,
    k_ref,
    v_ref,
    keys_ref,
    values_ref,
    fetched,
):
    here = pl.program_id(0)
    length = pick(facts_ref, here)[2]

    def fetch(i):
        row, doc, _ = pick(facts_ref, i)
        pairs = (
            (q_in.at[row], q_ref.at[i]),
            (keys_in.at[doc], keys_ref.at[i]),
            (k_in.at[row], k_ref.at[i]),
            (v_in.at[row], v_ref.at[i]),
            (values_in.at[doc], values_ref.at[i]),
        )
        return [pltpu.make_async_copy(a, b, fetched.at[i, n]) for n, (a, b) in enumerate(pairs)]

    @pl.when(jnp.logical_and(here == 0, length > 0))
    def _():
        for i in range(q_ref.shape[0]):
            for copy in fetch(i):
                copy.start()

    scale = HD ** (-0.5)
    steep = scale * LOG2E
    rows = q_ref.shape[1]
    along = (((1,), (1,)), ((), ()))
    across = (((0,), (0,)), ((), ()))
    block = KEY_BLOCK
    most = keys_ref.shape[1] // block
    blocks = lax.div(length + (block - 1), block)

    def over_rows(op, array):
        return op(array.reshape(-1, 8, rows), axis=0)

    def suffix(count):
        for copy in fetch(here):
            copy.wait()
        queries = q_ref[here]
        own = lax.dot_general(k_ref[here], queries, along, preferred_element_type=jnp.float32)
        token = lax.rem(lax.broadcasted_iota(jnp.int32, (SL, rows), 1), SL)
        other = lax.broadcasted_iota(jnp.int32, (SL, rows), 0)
        own = jnp.where(other <= token, own, MASKED)
        scores = []
        for b in range(count):
            keys = keys_ref[here, b * block : (b + 1) * block, :]
            score = lax.dot_general(keys, queries, along, preferred_element_type=jnp.float32)
            if b == count - 1:
                position = lax.broadcasted_iota(jnp.int32, (block, rows), 0) + b * block
                score = jnp.where(position < length, score, MASKED)
            scores.append(score)
        peak = functools.reduce(jnp.maximum, [over_rows(jnp.max, score) for score in scores])

        own_peak = jnp.max(own, axis=0, keepdims=True)
        own_weights = jnp.exp2((own - own_peak) * steep)
        own_total = jnp.sum(own_weights, axis=0, keepdims=True)
        own_out = lax.dot_general(
            v_ref[here], own_weights.astype(jnp.bfloat16), across, preferred_element_type=jnp.float32
        )

        peak = jnp.max(peak, axis=0, keepdims=True)
        total, acc = 0.0, 0.0
        for b in range(count):
            weights = jnp.exp2((scores[b] - peak) * steep)
            total += over_rows(jnp.sum, weights)
            acc += lax.dot_general(
                values_ref[here, b * block : (b + 1) * block, :],
                weights.astype(jnp.bfloat16),
                across,
                preferred_element_type=jnp.float32,
            )
        total = jnp.sum(total, axis=0, keepdims=True)
        prefix_normed = (acc * (1.0 / total)).astype(jnp.bfloat16)
        prefix_lse = peak * scale + jnp.log(total)
        own_peak = own_peak * scale
        top = jnp.maximum(prefix_lse, own_peak)
        former = jnp.exp(prefix_lse - top)
        latter = jnp.exp(own_peak - top)
        inverse = 1.0 / (former + own_total * latter)
        mixed = prefix_normed.astype(jnp.float32) * (former * inverse) + own_out * (latter * inverse)
        mixed = mixed.T.astype(jnp.bfloat16)
        for h in range(rows // SL):
            out_ref[:, h * HD : (h + 1) * HD] = mixed[h * SL : (h + 1) * SL, :]

    for count in range(1, most + 1):
        @pl.when(blocks == count)
        def _():
            suffix(count)


def attend(pick, count, facts, queries, own_keys, own_values, keys, values):
    rows = queries.shape[1]
    length = keys.shape[1]
    wide = rows // SL * HD
    far = pl.BlockSpec(memory_space=pltpu.HBM)
    held = pltpu.VMEM
    bf16 = jnp.bfloat16
    flops = 2 * count * rows * length * HD
    return pl.pallas_call(
        functools.partial(attend_kernel, pick),
        out_shape=jax.ShapeDtypeStruct((count * SL, wide), jnp.bfloat16),
        grid_spec=pltpu.PrefetchScalarGridSpec(
            num_scalar_prefetch=1,
            grid=(count,),
            in_specs=[far] * 5,
            out_specs=pl.BlockSpec((SL, wide), lambda i, facts: (i, 0)),
            scratch_shapes=[
                held((count, rows, HD), bf16),
                held((count, SL, HD), bf16),
                held((count, SL, HD), bf16),
                held((count, length, HD), bf16),
                held((count, length, HD), bf16),
                pltpu.SemaphoreType.DMA((count, 5)),
            ],
        ),
        compiler_params=pltpu.CompilerParams(
            dimension_semantics=("arbitrary",), vmem_limit_bytes=60 << 20
        ),
        cost_estimate=pl.CostEstimate(
            flops=flops, transcendentals=flops // (4 * HD), bytes_accessed=4 << 20
        ),
    )(facts, queries, own_keys, own_values, keys, values)


def place():
    c = lax.axis_index("corpus")
    f = lax.axis_index("fsdp")
    return c, lax.div(f, 2), lax.rem(f, 2)


def flip(value, bits):
    low = lax.rem(lax.rem(value, 2) + bits % 2, 2)
    high = lax.rem(lax.div(value, 2) + bits // 2, 2)
    return 2 * high + low


def remote(src, dst, send, recv, c, z, k):
    return pltpu.make_async_remote_copy(
        src_ref=src,
        dst_ref=dst,
        send_sem=send,
        recv_sem=recv,
        device_id=(c, 2 * z + k),
        device_id_type=MESH,
    )


def greet(peers):
    barrier = pltpu.get_barrier_semaphore()
    for c, z, k in peers:
        pl.semaphore_signal(barrier, inc=1, device_id=(c, 2 * z + k), device_id_type=MESH)
    pl.semaphore_wait(barrier, len(peers))


def move_kernel(
    x_ref,
    wq_ref,
    wk_ref,
    wv_ref,
    kc_ref,
    vc_ref,
    len_ref,
    doc_ref,
    gain_in,
    qb_in,
    kb_in,
    vb_in,
    ct_in,
    st_in,
    turn_in,
    out_ref,
    q_ref,
    ok_ref,
    ov_ref,
    keys_ref,
    values_ref,
    weights_ref,
    stat_ref,
    stage,
    numbers,
    facts_ref,
    acts,
    wbuf,
    normed,
    acc,
    cos_ref,
    sin_ref,
    facts_held,
    gain_ref,
    qb_ref,
    kb_ref,
    vb_ref,
    ct_ref,
    st_ref,
    turn_ref,
    start_ref,
    asend,
    arecv,
    xsend,
    xrecv,
    fsend,
    frecv,
    wsend,
    wrecv,
    wcsend,
    wcrecv,
    ksend,
    krecv,
    kcsend,
    kcrecv,
    osend,
    orecv,
    local,
):
    c, z, k = place()
    head = lax.div(z, 2)
    f = 2 * z + k
    length = kc_ref.shape[1]
    for r in range(4):
        facts_ref[r : r + 1, :] = jnp.full((1, HD), len_ref[r], jnp.int32)
        facts_ref[r + 4 : r + 5, :] = jnp.full((1, HD), doc_ref[r], jnp.int32)
    inner = jnp.logical_or(z == 1, z == 2)
    outer = jnp.logical_not(inner)
    greet(
        [(c, flip(z, s), k) for s in (1, 2, 3)]
        + [(flip(c, p), z, k) for p in (1, 2, 3)]
        + [(c, z, 1 - k)]
    )
    group = wq_ref.shape[1] // 2

    def act_to(s):
        return remote(x_ref, acts.at[z, c], asend.at[s - 1], arecv.at[s - 1], c, flip(z, s), k)

    def act_side(s, p):
        j = flip(z, s)
        src = x_ref if isinstance(s, int) and s == 0 else acts.at[j, c]
        return remote(src, acts.at[j, c], xsend.at[s, p - 1], xrecv.at[s, p - 1], flip(c, p), z, k)

    def fact_to(s):
        return remote(
            facts_ref, facts_held.at[z], fsend.at[s - 1], frecv.at[s - 1], c, flip(z, s), k
        )

    def weight_to(s, which_parts=(0, 1, 2)):
        to = flip(z, s)
        slot = wbuf.at[f]
        which = lax.div(to, 2)
        at = pl.multiple_of(which * group, group)
        kv = pl.multiple_of(which * HD, HD)
        parts = (
            (wk_ref.at[:, pl.ds(kv, HD)], slot.at[:, group : group + HD]),
            (wv_ref.at[:, pl.ds(kv, HD)], slot.at[:, group + HD : group + 2 * HD]),
            (wq_ref.at[:, pl.ds(at, group)], slot.at[:, 0:group]),
        )
        if s == 0:
            return [pltpu.make_async_copy(*parts[i], local.at[i]) for i in which_parts]
        return [
            remote(*parts[i], wsend.at[s - 1, i], wrecv.at[s - 1, i], c, to, k) for i in which_parts
        ]

    def weight_core(s):
        slot = wbuf.at[2 * flip(z, s) + k]
        return remote(slot, slot, wcsend.at[s], wcrecv.at[s], c, z, 1 - k)

    def piece(t):
        if t == 0:
            return kc_ref, keys_ref, slice(0, length)
        return vc_ref, values_ref, slice((t - 1) * length // 2, t * length // 2)

    def own_slice(t, which):
        cache, _, part = piece(t)
        return cache.at[0, part, pl.ds(pl.multiple_of(which * HD, HD), HD)]

    def kept(t, doc):
        _, buffer, part = piece(t)
        return buffer.at[doc, part, :]

    def kv_to(s, t):
        to = flip(z, s)
        return remote(
            own_slice(t, lax.div(to, 2)), kept(t, f), ksend.at[s - 1, t], krecv.at[s - 1, t], c, to, k
        )

    def kv_core(s, t):
        slot = kept(t, 2 * flip(z, s) + k)
        src = own_slice(t, head) if s == 0 else slot
        return remote(src, slot, kcsend.at[s, t], kcrecv.at[s, t], c, z, 1 - k)

    def kv_local(t):
        return pltpu.make_async_copy(own_slice(t, head), kept(t, f), local.at[13 + t])

    def rows_of(r, which):
        rows = pl.ds(pl.multiple_of(r * SL, SL), SL)
        return out_ref.at[rows, pl.ds(pl.multiple_of(which * group, group), group)]

    def out_to(s, r):
        return remote(
            stage.at[s, r], rows_of(r, head), osend.at[s, r], orecv.at[s, r], c, flip(z, s), k
        )

    def out_local(r):
        return pltpu.make_async_copy(stage.at[0, r], rows_of(r, head), osend.at[0, r])

    act_own = pltpu.make_async_copy(x_ref, acts.at[z, c], local.at[5])
    fact_own = pltpu.make_async_copy(facts_ref, facts_held.at[z], local.at[6])
    small = [
        pltpu.make_async_copy(a, b, local.at[i + (3 if i < 2 else 5)])
        for i, (a, b) in enumerate(
            (
                (gain_in, gain_ref),
                (qb_in, qb_ref),
                (kb_in, kb_ref),
                (vb_in, vb_ref),
                (ct_in, ct_ref),
                (st_in, st_ref),
                (turn_in, turn_ref),
            )
        )
    ]

    def project(s):
        j = flip(z, s)
        for p in (1, 2, 3):
            act_side(s, p).wait_recv()

        angle = facts_held[j].astype(jnp.float32) * turn_ref[0:1, :]
        start_ref[0] = jnp.cos(angle)
        start_ref[1] = jnp.sin(angle) * turn_ref[1:2, :]

        @pl.loop(0, 4)
        def _(r):
            at = pl.multiple_of(r * SL, SL)
            total = jnp.zeros((SL, 1), jnp.float32)
            for i in range(COLUMNS):
                wide = acts[j, i, pl.ds(at, SL), :].astype(jnp.float32)
                total += jnp.sum(wide * wide, axis=1, keepdims=True)
            inv = lax.rsqrt(total / (COLUMNS * acts.shape[3]) + EPS)
            for i in range(COLUMNS):
                wide = acts[j, i, pl.ds(at, SL), :].astype(jnp.float32)
                columns = pl.ds(i * acts.shape[3], acts.shape[3])
                normed[pl.ds(at, SL), columns] = (wide * inv * gain_ref[:, columns]).astype(jnp.bfloat16)
            cosl = start_ref[0, pl.ds(r, 1), :]
            sinl = start_ref[1, pl.ds(r, 1), :]
            cos_ref[pl.ds(at, SL), :] = cosl * ct_ref[...] - sinl * st_ref[...]
            sin_ref[pl.ds(at, SL), :] = sinl * ct_ref[...] + cosl * st_ref[...]

        @pl.loop(0, acc.shape[1] // WIDE)
        def _(i):
            columns = pl.ds(pl.multiple_of(i * WIDE, WIDE), WIDE)
            part = wbuf[:, :, columns].reshape(-1, WIDE)
            acc[:, columns] = jnp.dot(normed[...], part, preferred_element_type=jnp.float32)

        cosine, sine = cos_ref[...], sin_ref[...]
        heads = group // HD
        for h in range(heads):
            lin = acc[:, h * HD : (h + 1) * HD] + qb_ref[pl.ds(heads * head + h, 1), :]
            turned = rotate(lin, cosine, sine).astype(jnp.bfloat16)
            for i in range(4):
                q_ref[4 * j + i, h * SL : (h + 1) * SL, :] = turned[i * SL : (i + 1) * SL]
        lin = acc[:, group : group + HD] + kb_ref[pl.ds(head, 1), :]
        turned = rotate(lin, cosine, sine).astype(jnp.bfloat16)
        straight = (acc[:, group + HD : group + 2 * HD] + vb_ref[pl.ds(head, 1), :]).astype(jnp.bfloat16)
        for i in range(4):
            ok_ref[4 * j + i] = turned[i * SL : (i + 1) * SL]
            ov_ref[4 * j + i] = straight[i * SL : (i + 1) * SL]

    scale = HD ** (-0.5)
    steep = scale * LOG2E
    rows = q_ref.shape[1]
    along = (((1,), (1,)), ((), ()))
    across = (((0,), (0,)), ((), ()))
    cuts = [slice(at, at + KEY_BLOCK) for at in range(0, length, KEY_BLOCK)]

    def over_rows(op, array):
        return op(array.reshape(-1, 8, rows), axis=0)

    def weigh(s, r, slot):
        j = flip(z, s)
        doc, size = numbers[j, 4 + r, 0], numbers[j, r, 0]
        queries = q_ref[4 * j + r]
        scores = []
        for cut in cuts:
            score = lax.dot_general(
                keys_ref[doc, cut, :], queries, along, preferred_element_type=jnp.float32
            )
            position = lax.broadcasted_iota(jnp.int32, score.shape, 0)
            scores.append(jnp.where(position < size - cut.start, score, MASKED))
        peak = functools.reduce(jnp.maximum, [over_rows(jnp.max, score) for score in scores])
        peak = jnp.max(peak, axis=0, keepdims=True)
        total = 0.0
        for score, cut in zip(scores, cuts):
            weights = jnp.exp2((score - peak) * steep)
            total += over_rows(jnp.sum, weights)
            weights_ref[slot, cut, :] = weights.astype(jnp.bfloat16)
        stat_ref[slot, 0:1, :] = peak * scale
        stat_ref[slot, 1:2, :] = jnp.sum(total, axis=0, keepdims=True)

    def blend(s, r, slot):
        j = flip(z, s)
        doc = numbers[j, 4 + r, 0]
        row = 4 * j + r
        own = lax.dot_general(ok_ref[row], q_ref[row], along, preferred_element_type=jnp.float32)
        token = lax.rem(lax.broadcasted_iota(jnp.int32, (SL, rows), 1), SL)
        other = lax.broadcasted_iota(jnp.int32, (SL, rows), 0)
        own = jnp.where(other <= token, own, MASKED)
        acc = 0.0
        for cut in cuts:
            acc += lax.dot_general(
                values_ref[doc, cut, :],
                weights_ref[slot, cut, :],
                across,
                preferred_element_type=jnp.float32,
            )
        own_peak = jnp.max(own, axis=0, keepdims=True)
        own_weights = jnp.exp2((own - own_peak) * steep)
        own_total = jnp.sum(own_weights, axis=0, keepdims=True)
        own_out = lax.dot_general(
            ov_ref[row], own_weights.astype(jnp.bfloat16), across, preferred_element_type=jnp.float32
        )
        total = stat_ref[slot, 1:2, :]
        prefix_normed = (acc * (1.0 / total)).astype(jnp.bfloat16)
        prefix_lse = stat_ref[slot, 0:1, :] + jnp.log(total)
        own_peak = own_peak * scale
        top = jnp.maximum(prefix_lse, own_peak)
        former = jnp.exp(prefix_lse - top)
        latter = jnp.exp(own_peak - top)
        inverse = 1.0 / (former + own_total * latter)
        mixed = prefix_normed.astype(jnp.float32) * (former * inverse) + own_out * (latter * inverse)
        mixed = mixed.T.astype(jnp.bfloat16)
        for h in range(rows // SL):
            stage[s, r, :, h * HD : (h + 1) * HD] = mixed[h * SL : (h + 1) * SL, :]

    @pl.when(outer)
    def _():
        for s in (2, 1):
            act_to(s).start()
        for s in (1, 2, 3):
            fact_to(s).start()
        fact_own.start()
        for s in (2, 1):
            for copy in weight_to(s, (0, 1)):
                copy.start()
        for s in (2, 1):
            act_to(s).wait_send()
            weight_to(s, (2,))[0].start()
        for t in PIECES:
            for s in (2, 1):
                if t == 0:
                    weight_to(s, (2,))[0].wait_send()
                else:
                    kv_to(s, t - 1).wait_send()
                kv_to(s, t).start()
        for s in (1, 2, 3):
            fact_to(s).wait()
        fact_own.wait()
        for s in (2, 1):
            for copy in weight_to(s, (0, 1)):
                copy.wait_send()
            kv_to(s, PIECES[-1]).wait_send()
        for s in (2, 1):
            for r in range(4):
                out_to(s, r).wait_recv()

    @pl.when(inner)
    def _():
        act_to(3).start()
        for s in (1, 2, 3):
            fact_to(s).start()
        fact_own.start()
        for p in (1, 2, 3):
            act_side(0, p).start()
        act_own.start()
        for copy in weight_to(0):
            copy.start()
        for copy in weight_to(3, (0, 1)):
            copy.start()
        for copy in small:
            copy.start()
        for t in PIECES:
            kv_local(t).start()
            kv_core(0, t).start()
        act_to(3).wait_send()
        weight_to(3, (2,))[0].start()
        for s in (1, 3, 2):
            act_to(s).wait_recv()
            for p in (1, 2, 3):
                act_side(s, p).start()
        for copy in weight_to(0):
            copy.wait()
        weight_core(0).start()
        for s in (1, 3):
            for copy in weight_to(s):
                copy.wait_recv()
            weight_core(s).start()
        for copy in weight_to(3):
            copy.wait_send()
        for t in PIECES:
            kv_to(3, t).start()
        for copy in weight_to(2):
            copy.wait_recv()
        weight_core(2).start()

        for s in (1, 2, 3):
            fact_to(s).wait()
        fact_own.wait()
        to_scalars = pltpu.make_async_copy(facts_held, numbers, local.at[6])
        to_scalars.start()
        act_own.wait()
        for copy in small:
            copy.wait()
        for s in range(4):
            weight_core(s).wait_recv()

        @pl.loop(0, LINES)
        def _(i):
            project(jnp.where(i < 2, i, 5 - i))

        to_scalars.wait()
        kv_to(3, 0).wait_send()

        def pass_on(t):
            for s in (1, 3, 2):
                kv_to(s, t).wait_recv()
                kv_core(s, t).start()

        def arrived(t):
            kv_local(t).wait()
            for s in range(4):
                kv_core(s, t).wait_recv()

        pass_on(0)
        arrived(0)

        @pl.loop(0, 8)
        def _(n):
            weigh(2 + lax.div(n, 4), lax.rem(n, 4), n)

        for t in PIECES[1:]:
            pass_on(t)
        for t in PIECES[1:]:
            arrived(t)

        @pl.loop(0, 8)
        def _(n):
            s, r = 2 + lax.div(n, 4), lax.rem(n, 4)
            blend(s, r, n)
            out_to(s, r).start()

        @pl.loop(0, 8)
        def _(n):
            s, r = 1 - lax.div(n, 4), lax.rem(n, 4)
            weigh(s, r, n)
            blend(s, r, n)

            @pl.when(s == 1)
            def _():
                out_to(1, r).start()

            @pl.when(s == 0)
            def _():
                out_local(r).start()

        act_sides = [act_side(s, p) for s in range(4) for p in (1, 2, 3)]
        for copy in act_sides:
            copy.wait_send()
        for s in range(4):
            weight_core(s).wait_send()
        for t in PIECES:
            if t:
                kv_to(3, t).wait_send()
            for s in range(4):
                kv_core(s, t).wait_send()
        for r in range(4):
            out_local(r).wait()
            for s in (1, 2, 3):
                out_to(s, r).wait_send()
            out_to(3, r).wait_recv()


def move(inputs, w_query, w_key, w_value, key_cache, value_cache, prefix_len, source_doc, *small):
    tokens, wide = inputs.shape
    depth = w_query.shape[0]
    group = w_query.shape[1] // 2
    length = key_cache.shape[1]
    docs = 2 * LINES
    suffixes = LINES * (tokens // SL)
    rows = group // HD * SL
    far = pl.BlockSpec(memory_space=pltpu.HBM)
    dma = pltpu.SemaphoreType.DMA
    bf16, f32 = jnp.bfloat16, jnp.float32
    facts = (2 * prefix_len.shape[0], HD)
    scalars = pl.BlockSpec(memory_space=pltpu.SMEM)
    flops = 2 * LINES * tokens * wide * COLUMNS * (group + 2 * HD)
    return pl.pallas_call(
        move_kernel,
        out_shape=jax.ShapeDtypeStruct((tokens, 2 * group), bf16),
        in_specs=[far] * 6 + [scalars] * 2 + [far] * len(small),
        out_specs=far,
        scratch_shapes=[
            pltpu.VMEM((suffixes, rows, HD), bf16),
            pltpu.VMEM((suffixes, SL, HD), bf16),
            pltpu.VMEM((suffixes, SL, HD), bf16),
            pltpu.VMEM((docs, length, HD), bf16),
            pltpu.VMEM((docs, length, HD), bf16),
            pltpu.VMEM((8, length, rows), bf16),
            pltpu.VMEM((8, 8, rows), f32),
            pltpu.VMEM((LINES, tokens // SL, SL, group), bf16),
            pltpu.SMEM((LINES,) + facts, jnp.int32),
            pltpu.VMEM(facts, jnp.int32),
            pltpu.VMEM((LINES, COLUMNS, tokens, wide), bf16),
            pltpu.VMEM((docs, depth, group + 2 * HD), bf16),
            pltpu.VMEM((tokens, wide * COLUMNS), bf16),
            pltpu.VMEM((tokens, group + 2 * HD), f32),
            pltpu.VMEM((tokens, HD), f32),
            pltpu.VMEM((tokens, HD), f32),
            pltpu.VMEM((LINES,) + facts, jnp.int32),
            *[pltpu.VMEM(array.shape, f32) for array in small],
            pltpu.VMEM((2,) + facts, f32),
            dma((3,)),
            dma((3,)),
            dma((4, 3)),
            dma((4, 3)),
            dma((3,)),
            dma((3,)),
            dma((3, 3)),
            dma((3, 3)),
            dma((4,)),
            dma((4,)),
            dma((3, 3)),
            dma((3, 3)),
            dma((4, 3)),
            dma((4, 3)),
            dma((4, 4)),
            dma((4, 4)),
            dma((16,)),
        ],
        compiler_params=pltpu.CompilerParams(
            collective_id=0, has_side_effects=True, vmem_limit_bytes=62 << 20
        ),
        cost_estimate=pl.CostEstimate(flops=flops, transcendentals=0, bytes_accessed=32 << 20),
    )(inputs, w_query, w_key, w_value, key_cache, value_cache, prefix_len, source_doc, *small)


def heads_by_line(
    inputs,
    norm_gain,
    w_query,
    w_key,
    w_value,
    query_bias,
    key_bias,
    value_bias,
    key_cache,
    value_cache,
    source_doc,
    prefix_len,
):
    freq = THETA ** (-(np.arange(HD // 2) * 2.0 / HD))
    sign = np.repeat([-1.0, 1.0], HD // 2)
    freq = np.tile(freq, 2)
    step = np.arange(SL)[:, None] * freq
    tables = (np.cos(step), np.sin(step) * sign, np.stack([freq, sign]))
    return move(
        inputs,
        w_query,
        w_key,
        w_value,
        key_cache,
        value_cache,
        prefix_len,
        source_doc,
        norm_gain[None],
        query_bias.reshape(-1, HD),
        key_bias.reshape(-1, HD),
        value_bias.reshape(-1, HD),
        *[jnp.asarray(table, jnp.float32) for table in tables],
    )


def dense_attend(source_doc, prefix_len, q_lin, k_lin, v_lin, cosine, sine, keys, values):
    suffixes = source_doc.shape[0]
    kv_heads = k_lin.shape[1] // HD
    group = q_lin.shape[1] // k_lin.shape[1]

    def turned(lin):
        vector = lin.reshape(suffixes * SL, -1, HD)
        other = jnp.roll(vector, HD // 2, axis=-1)
        return (vector * cosine[:, None] + other * sine[:, None]).astype(jnp.bfloat16)

    queries = turned(q_lin).reshape(suffixes, SL, kv_heads, group, HD)
    queries = queries.transpose(0, 2, 3, 1, 4).reshape(suffixes * kv_heads, group * SL, HD)
    own_keys = turned(k_lin).reshape(suffixes, SL, kv_heads, HD).swapaxes(1, 2).reshape(-1, SL, HD)
    own_values = v_lin.astype(jnp.bfloat16)
    own_values = own_values.reshape(suffixes, SL, kv_heads, HD).swapaxes(1, 2).reshape(-1, SL, HD)

    def by_head(cache):
        return cache.reshape(-1, cache.shape[1], kv_heads, HD).swapaxes(1, 2).reshape(-1, cache.shape[1], HD)

    docs = (source_doc[:, None] * kv_heads + jnp.arange(kv_heads, dtype=jnp.int32)[None, :]).reshape(-1)
    lengths = jnp.repeat(prefix_len, kv_heads)
    facts = jnp.stack([docs, lengths])
    pick = lambda facts_ref, i: (i, facts_ref[0, i], facts_ref[1, i])
    out = attend(pick, docs.shape[0], facts, queries, own_keys, own_values, by_head(keys), by_head(values))
    out = out.reshape(suffixes, kv_heads, SL, group * HD).swapaxes(1, 2)
    return out.reshape(suffixes * SL, kv_heads * group * HD)


def gather_all(
    inputs,
    norm_gain,
    w_query,
    w_key,
    w_value,
    query_bias,
    key_bias,
    value_bias,
    key_cache,
    value_cache,
    source_doc,
    prefix_len,
):
    full_rows = lax.all_gather(inputs, "corpus", axis=1, tiled=True)
    normed = normalize(full_rows, norm_gain)

    def project(weight, bias):
        whole = lax.all_gather(weight, "fsdp", axis=0, tiled=True)
        return jnp.dot(normed, whole, preferred_element_type=jnp.float32) + bias

    q_lin, k_lin, v_lin = project(w_query, query_bias), project(w_key, key_bias), project(w_value, value_bias)
    keys = lax.all_gather(key_cache, "fsdp", axis=0, tiled=True)
    values = lax.all_gather(value_cache, "fsdp", axis=0, tiled=True)
    position = prefix_len[:, None] + jnp.arange(SL, dtype=jnp.int32)[None, :]
    cosine, sine = rope_tables(position.reshape(-1), HD)
    return dense_attend(source_doc, prefix_len, q_lin, k_lin, v_lin, cosine, sine, keys, values)


def shards(*arrays):
    fits = (
        lax.axis_size("fsdp") == 2 * LINES
        and lax.axis_size("corpus") == COLUMNS
        and arrays[2].shape[1] == LINES * 4 * HD
        and arrays[3].shape[1] == 2 * HD
    )
    return heads_by_line(*arrays) if fits else gather_all(*arrays)


def solution(mesh):
    in_specs = (
        P("fsdp", "corpus"),
        P(),
        P("fsdp", "corpus"),
        P("fsdp", "corpus"),
        P("fsdp", "corpus"),
        P("corpus"),
        P("corpus"),
        P("corpus"),
        P("fsdp", None, "corpus"),
        P("fsdp", None, "corpus"),
        P("fsdp"),
        P("fsdp"),
    )
    out_specs = P("fsdp", "corpus")
    return jax.shard_map(shards, mesh=mesh, in_specs=in_specs, out_specs=out_specs, check_vma=False)
```
